128 devices in a mesh: blk: 8 (over z_lo, x), grp: 16 (over y, z_hi, core).
Axes of the slice: x: 4, y: 4, z: 4 (z_hi: 2, z_lo: 2; z = z_hi * 2 + z_lo), core: 2. Of those that a mesh axis runs over, the one named last changes fastest.
Arguments:
- a_blocks: bfloat16 [16, 192, 27, 96, 96], P('grp', 'blk'), may hold values from -0.125 to 0.125
- col_index: int32 [16, 192, 27], P('grp', 'blk'), may hold values from 0 to 191
- prolong: bfloat16 [16, 192, 2, 96, 96], P('grp', 'blk'), may hold values from -0.625 to 0.625
- target: int32 [16, 192, 108], P('grp', 'blk'), may hold values from 0 to 511
Outputs:
- coarse: float32 [16, 32, 96, 96], P('grp', 'blk')
The draws below stay inside these ranges and needn't reach their ends.
All inputs are finite; a program needn't handle non-finite values.
Results may differ from the reference program's by a relative error of at most 0.0029.
Values may be sent and summed in bfloat16 or wider, within the bound.
A program may use at most 320 MiB of HBM per device.

```python
import math
import jax
import jax.numpy as jnp
from jax import lax

B = 96
KA = 27
KP = 2
FR = 24
GROUPS = 16
FINE_G = 192
COARSE_G = 32


def draw_col_index(key, part):
    shape = (GROUPS, FINE_G, KA)
    key_near = jax.random.fold_in(key, 11)
    key_far = jax.random.fold_in(key, 12)
    key_kind = jax.random.fold_in(key, 13)
    row_ids = jnp.arange(FINE_G, dtype=jnp.int32)[None, :, None]
    offset = jax.random.randint(key_near, shape, -FR, FR + 1, dtype=jnp.int32)
    near_col = jnp.mod(row_ids + offset, FINE_G)
    far_col = jax.random.randint(key_far, shape, 0, FINE_G, dtype=jnp.int32)
    kind = jax.random.randint(key_kind, shape, 0, 5, dtype=jnp.int32)
    return jnp.where(kind == 0, far_col, near_col).astype(jnp.int32)


def draw_target(key, part):
    shape = (GROUPS, FINE_G, KP * KA * KP)
    key_kind = jax.random.fold_in(key, 21)
    key_slot = jax.random.fold_in(key, 22)
    key_far = jax.random.fold_in(key, 23)
    group_ids = jnp.arange(GROUPS, dtype=jnp.int32)[:, None, None]
    kind = jax.random.randint(key_kind, shape, 0, 10, dtype=jnp.int32)
    slot = jax.random.randint(key_slot, shape, 0, COARSE_G, dtype=jnp.int32)
    far_target = jax.random.randint(key_far, shape, 0, GROUPS * COARSE_G, dtype=jnp.int32)
    owner = jnp.where(kind == 1, group_ids - 1, jnp.where(kind == 2, group_ids + 1, group_ids))
    owner = jnp.clip(owner, 0, GROUPS - 1)
    near_target = owner * COARSE_G + slot
    return jnp.where(kind == 0, far_target, near_target).astype(jnp.int32)


def levels(key, extent, pieces, low, high):
    loudness = 1.0
    for axis_at, shards_of in pieces:
        heights = jax.random.uniform(jax.random.fold_in(jax.random.fold_in(key, 6), axis_at), (shards_of,), jnp.float32, low / len(pieces), high / len(pieces))
        loudness = loudness * jnp.repeat(jnp.exp(heights), extent[axis_at] // shards_of).reshape((-1,) + (1,) * (len(extent) - 1 - axis_at))
    return loudness


def gaussian(key, dims, deviation, limit, pieces=(), kind=jnp.bfloat16):
    factor_of = levels(key, dims, pieces, -0.22, 0.18) if pieces else 1.0
    result = jax.random.normal(key, dims, jnp.float32) * deviation * factor_of
    return jnp.minimum(jnp.maximum(result, -limit), limit).astype(kind)


def setup_inputs(seed: int = 0) -> dict:
    seeds = jax.random.split(jax.random.key(seed), 5)
    a_blocks = gaussian(seeds[0], (GROUPS, FINE_G, KA, B, B), (KA * B) ** -0.5, 0.125, ((0, 16), (1, 8)))
    col_index = draw_col_index(jax.random.fold_in(seeds[4], 71), 0)
    prolong = gaussian(seeds[2], (GROUPS, FINE_G, KP, B, B), B ** -0.5, 0.625, ((0, 16), (1, 8)))
    target = draw_target(jax.random.fold_in(seeds[4], 71), 0)
    return {"a_blocks": a_blocks, "col_index": col_index, "prolong": prolong, "target": target}


def reference(a_blocks, col_index, prolong, target):
    slots = GROUPS * COARSE_G
    step = math.gcd(FINE_G, 16)

    def group_term(total, group):
        a_group = a_blocks[group]
        c_group = col_index[group]
        p_group = prolong[group]
        t_group = target[group]

        def rows_term(accum, low):
            a_part = lax.dynamic_slice_in_dim(a_group, low, step, 0).astype(jnp.float32)
            c_part = lax.dynamic_slice_in_dim(c_group, low, step, 0).astype(jnp.int32)
            p_part = lax.dynamic_slice_in_dim(p_group, low, step, 0).astype(jnp.float32)
            t_part = lax.dynamic_slice_in_dim(t_group, low, step, 0).astype(jnp.int32)
            chosen = jnp.take(p_group, c_part, axis=0).astype(jnp.float32)
            product = jnp.einsum("rkab,rkmbc->rkmac", a_part, chosen).astype(jnp.bfloat16)
            product = lax.optimization_barrier(product).astype(jnp.float32)
            partial_value = jnp.einsum("rnba,rkmbc->rnkmac", p_part, product)
            partial_value = partial_value.reshape(-1, B, B)
            accum = accum + jax.ops.segment_sum(partial_value, t_part.reshape(-1), num_segments=slots)
            return accum, None

        starts = jnp.arange(0, FINE_G, step, dtype=jnp.int32)
        total, _ = lax.scan(rows_term, total, starts)
        return total, None

    init = jnp.zeros((slots, B, B), jnp.float32)
    total, _ = lax.scan(group_term, init, jnp.arange(GROUPS, dtype=jnp.int32))
    return total.reshape(GROUPS, COARSE_G, B, B)
```

```python
import functools

import jax
import jax.numpy as jnp
from jax import lax
from jax.experimental import pallas as pl
from jax.experimental.pallas import tpu as pltpu
from jax.sharding import PartitionSpec as P

f32, bf16 = jnp.float32, jnp.bfloat16
MESH = pl.DeviceIdType.MESH

B = 96
LANES = 128
PACK = 72
KP = 2
KA = 27
FR = 24
MEMBERS = 8
GROUPS = 16
OWN = 4
SLOTS = 512
PARTS = 6
PIECE = OWN * PACK // PARTS
STEPS = 6
WIDE_FROM = 2

BITS = ("xg", "yg", "zg", "xh", "yh", "zh")


def bits_of(grp, blk):
    x, zl = blk % 4, blk // 4
    y, zh, core = grp // 4, (grp // 2) % 2, grp % 2
    xh, yh = x // 2, y // 2
    return {
        "xg": (xh + x % 2) % 2, "yg": (yh + y % 2) % 2, "zg": (zh + zl) % 2,
        "xh": xh, "yh": yh, "zh": zh, "core": core,
    }


def partner_of(grp, blk, bit):
    x, zl = blk % 4, blk // 4
    y, zh, core = grp // 4, (grp // 2) % 2, grp % 2
    if bit == "xg":
        x = x + 1 - 2 * (x % 2)
    elif bit == "xh":
        x = 3 - x
    elif bit == "yg":
        y = y + 1 - 2 * (y % 2)
    elif bit == "yh":
        y = 3 - y
    elif bit in ("zg", "zl"):
        zl = 1 - zl
    elif bit == "zh":
        zl, zh = 1 - zl, 1 - zh
    elif bit == "core":
        core = 1 - core
    return {"blk": zl * 4 + x, "grp": y * 4 + zh * 2 + core}


def order_of(part):
    return [BITS[(part + step) % STEPS] for step in range(STEPS)]


def enter(partners):
    barrier = pltpu.get_barrier_semaphore()
    for device in partners:
        pl.semaphore_signal(barrier, inc=1, device_id=device, device_id_type=MESH)
    pl.semaphore_wait(barrier, len(partners))


def fold(main, tail):
    lane = lax.broadcasted_iota(jnp.int32, main.shape, 1)
    side = jnp.concatenate([pltpu.roll(tail, shift, 1) for shift in (96, 64, 32)], axis=0)
    return jnp.where(lane < B, main, side)


def unfold(packed):
    n = packed.shape[0] // 3
    lane = lax.broadcasted_iota(jnp.int32, (n, LANES), 1)
    first = pltpu.roll(packed[:n], 32, 1)
    second = pltpu.roll(packed[n:2 * n], 64, 1)
    third = pltpu.roll(packed[2 * n:], 96, 1)
    return jnp.where(lane < 32, first, jnp.where(lane < 64, second, third))


G_ORDERS = (("xg", "xh", "zl"), ("xh", "zl", "xg"), ("zl", "xg", "xh"))
G_ROWS = FR // 3


def member_index(part, blk):
    x, zl = blk % 4, blk // 4
    xh = x // 2
    bits = {"xg": (xh + x % 2) % 2, "xh": xh, "zl": zl}
    return sum(bits[bit] * (1 << i) for i, bit in enumerate(G_ORDERS[part]))


def gather_kernel(p_ref, out_ref, mine, local_sem, send_sem, recv_sem):
    grp, blk = lax.axis_index("grp"), lax.axis_index("blk")
    partners = {bit: partner_of(grp, blk, bit) for bit in G_ORDERS[0]}
    for part in range(3):
        def pack(r, _):
            v = p_ref[part * G_ROWS + r].astype(f32)
            v = jnp.pad(v.reshape(KP * B, B), ((0, 0), (0, LANES - B)))
            mine[part, r] = fold(v[:2 * PACK], v[2 * PACK:]).astype(bf16)
            return 0
        lax.fori_loop(0, G_ROWS, pack, 0)
    enter(list(partners.values()))
    index = [member_index(part, blk) for part in range(3)]
    local = []
    for part in range(3):
        copy = pltpu.make_async_copy(mine.at[part], out_ref.at[part, index[part]], local_sem.at[part])
        copy.start()
        local.append(copy)
    sends = []
    for step in range(3):
        size = 1 << step
        current = []
        for part in range(3):
            if step == 1:
                local[part].wait()
            base = index[part] // size * size
            block = out_ref.at[part, pl.ds(base, size)]
            copy = pltpu.make_async_remote_copy(
                src_ref=mine.at[pl.ds(part, 1)] if step == 0 else block,
                dst_ref=block,
                send_sem=send_sem.at[step, part], recv_sem=recv_sem.at[step, part],
                device_id=partners[G_ORDERS[part][step]], device_id_type=MESH)
            if step:
                sends[-3].wait_recv()
            copy.start()
            sends.append(copy)
    for copy in sends[-3:]:
        copy.wait_recv()
    for copy in sends:
        copy.wait_send()


def gather(prolong):
    return pl.pallas_call(
        gather_kernel,
        out_shape=jax.ShapeDtypeStruct((3, MEMBERS, G_ROWS, 2 * PACK, LANES), bf16),
        in_specs=[pl.BlockSpec(memory_space=pltpu.VMEM)],
        out_specs=pl.BlockSpec(memory_space=pl.ANY),
        scratch_shapes=[
            pltpu.VMEM((3, G_ROWS, 2 * PACK, LANES), bf16),
            pltpu.SemaphoreType.DMA((3,)), pltpu.SemaphoreType.DMA((3, 3)), pltpu.SemaphoreType.DMA((3, 3))],
        compiler_params=pltpu.CompilerParams(collective_id=0, has_side_effects=True, vmem_limit_bytes=32 << 20),
        name="gather_prolong",
    )(prolong)


def product_kernel(col, tgt, a_ref, p_ref, g_ref, out_ref, raw, chosen, acc, p_trans, stage, g_sem, out_sem):
    i = pl.program_id(0)

    @pl.when(i == 0)
    def _():
        copies = [
            [pltpu.make_async_copy(g_ref.at[part, m], raw.at[part, m], g_sem.at[part, m]) for m in range(MEMBERS)]
            for part in range(3)]
        for row in copies:
            for copy in row:
                copy.start()

        @pl.loop(0, SLOTS)
        def _(s):
            acc[s] = jnp.zeros((B, LANES), f32)

        for part in range(3):
            for blk in range(MEMBERS):
                m = member_index(part, blk)
                copies[part][m].wait()

                def unpack(r, _):
                    packed = raw[part, m, r].astype(f32)
                    both = jnp.concatenate([packed, unfold(packed)], axis=0)
                    row = blk * FR + part * G_ROWS + r
                    for n in range(KP):
                        chosen[row, :, n * LANES:(n + 1) * LANES] = both[n * B:(n + 1) * B].astype(bf16)
                    return 0
                lax.fori_loop(0, G_ROWS, unpack, 0)

    for n in range(KP):
        p_trans[n * B:(n + 1) * B, :] = p_ref[0, n].T
    pt = p_trans[...]
    for k in range(KA):
        c = chosen[col[i * KA + k]]
        ap = jnp.dot(a_ref[0, k], c, preferred_element_type=f32).astype(bf16)
        value = jnp.dot(pt, ap, preferred_element_type=f32)
        for n in range(KP):
            for m in range(KP):
                slot = tgt[i * (KP * KA * KP) + n * (KA * KP) + k * KP + m]
                acc[slot] += value[n * B:(n + 1) * B, m * LANES:(m + 1) * LANES]

    @pl.when(i == pl.num_programs(0) - 1)
    def _():
        def flush(d, _):
            bits = bits_of(d // MEMBERS, d % MEMBERS)
            for pair in range(2):
                packed = []
                for j in range(2):
                    block = acc[d * OWN + pair * 2 + j]
                    packed.append(fold(block[:PACK], block[PACK:]))
                both = jnp.concatenate(packed, axis=0).astype(bf16)
                for piece in range(3):
                    part = pair * 3 + piece
                    entry = 0
                    for bit in order_of(part):
                        entry = entry * 2 + bits[bit]
                    stage[part, bits["core"], entry] = both[piece * PIECE:(piece + 1) * PIECE]
            return 0
        lax.fori_loop(0, GROUPS * MEMBERS, flush, 0)
        copy = pltpu.make_async_copy(stage, out_ref, out_sem)
        copy.start()
        copy.wait()


def products(a_rows, columns, p_rows, gathered, targets):
    stage = (PARTS, 2, 64, PIECE, LANES)
    return pl.pallas_call(
        product_kernel,
        out_shape=jax.ShapeDtypeStruct(stage, bf16),
        grid_spec=pltpu.PrefetchScalarGridSpec(
            num_scalar_prefetch=2, grid=(FR,),
            in_specs=[
                pl.BlockSpec((1, KA, B, B), lambda i, *_: (i, 0, 0, 0)),
                pl.BlockSpec((1, KP, B, B), lambda i, *_: (i, 0, 0, 0)),
                pl.BlockSpec(memory_space=pl.ANY)],
            out_specs=pl.BlockSpec(memory_space=pl.ANY),
            scratch_shapes=[
                pltpu.VMEM((3, MEMBERS, G_ROWS, 2 * PACK, LANES), bf16),
                pltpu.VMEM((FR * MEMBERS, B, KP * LANES), bf16),
                pltpu.VMEM((SLOTS, B, LANES), f32),
                pltpu.VMEM((KP * B, B), bf16),
                pltpu.VMEM(stage, bf16),
                pltpu.SemaphoreType.DMA((3, MEMBERS)), pltpu.SemaphoreType.DMA]),
        compiler_params=pltpu.CompilerParams(vmem_limit_bytes=60 << 20),
        name="products",
    )(columns.reshape(-1), targets.reshape(-1), a_rows, p_rows, gathered)


def wire(step):
    return f32 if step >= WIDE_FROM else bf16


def scatter_kernel(in_ref, out_ref, *refs):
    refs = list(refs)
    own, other = refs.pop(0), refs.pop(0)
    keep = [refs.pop(0) for _ in range(STEPS)]
    give = [refs.pop(0) for _ in range(STEPS)]
    got = [refs.pop(0) for _ in range(STEPS)]
    own_sem, core_send, core_recv, send_sem, recv_sem = refs
    grp, blk = lax.axis_index("grp"), lax.axis_index("blk")
    bits = bits_of(grp, blk)
    partners = {bit: partner_of(grp, blk, bit) for bit in BITS + ("core",)}
    core = bits["core"]
    local = []
    for part in range(PARTS):
        copy = pltpu.make_async_copy(in_ref.at[part, core], own.at[part], own_sem.at[part])
        copy.start()
        local.append(copy)
    enter(list(partners.values()))
    crossed = []
    for part in range(PARTS):
        copy = pltpu.make_async_remote_copy(
            src_ref=in_ref.at[part, 1 - core], dst_ref=other.at[part],
            send_sem=core_send.at[part], recv_sem=core_recv.at[part],
            device_id=partners["core"], device_id_type=MESH)
        copy.start()
        crossed.append(copy)
    sends = [[None] * PARTS for _ in range(STEPS)]
    for step in range(STEPS):
        half = 32 >> step
        for part in range(PARTS):
            bit = order_of(part)[step]
            away, here = (1 - bits[bit]) * half, bits[bit] * half
            if step == 0:
                local[part].wait()
                crossed[part].wait_recv()
                first, second = own, other
            else:
                sends[step - 1][part].wait_recv()
                first, second = keep[step - 1], got[step - 1]

            def combine(offset, target, dtype):
                def one(e, _):
                    total = first[part, offset + e].astype(f32) + second[part, offset + e].astype(f32)
                    target[part, e] = total.astype(dtype)
                    return 0
                lax.fori_loop(0, half, one, 0)

            combine(away, give[step], wire(step))
            copy = pltpu.make_async_remote_copy(
                src_ref=give[step].at[part], dst_ref=got[step].at[part],
                send_sem=send_sem.at[step, part], recv_sem=recv_sem.at[step, part],
                device_id=partners[bit], device_id_type=MESH)
            copy.start()
            sends[step][part] = copy
            combine(here, keep[step], f32)
    pieces = []
    for part in range(PARTS):
        sends[-1][part].wait_recv()
        pieces.append(keep[-1][part, 0] + got[-1][part, 0])
    for pair in range(2):
        both = jnp.concatenate(pieces[pair * 3:pair * 3 + 3], axis=0)
        for j in range(2):
            packed = both[j * PACK:(j + 1) * PACK]
            out_ref[0, pair * 2 + j, :PACK] = packed[:, :B]
            out_ref[0, pair * 2 + j, PACK:] = unfold(packed)[:, :B]
    for copy in crossed:
        copy.wait_send()
    for row in sends:
        for copy in row:
            copy.wait_send()


def scatter(staged):
    halves = [32 >> step for step in range(STEPS)]
    return pl.pallas_call(
        scatter_kernel,
        out_shape=jax.ShapeDtypeStruct((1, OWN, B, B), f32),
        in_specs=[pl.BlockSpec(memory_space=pl.ANY)],
        out_specs=pl.BlockSpec(memory_space=pltpu.VMEM),
        scratch_shapes=(
            [pltpu.VMEM((PARTS, 64, PIECE, LANES), bf16)] * 2
            + [pltpu.VMEM((PARTS, n, PIECE, LANES), f32) for n in halves]
            + [pltpu.VMEM((PARTS, n, PIECE, LANES), wire(s)) for s, n in enumerate(halves)] * 2
            + [pltpu.SemaphoreType.DMA((PARTS,))] * 3
            + [pltpu.SemaphoreType.DMA((STEPS, PARTS))] * 2),
        compiler_params=pltpu.CompilerParams(collective_id=1, has_side_effects=True, vmem_limit_bytes=48 << 20),
        name="sum_at_owners",
    )(staged)


def shards(a_blocks, col_index, prolong, target):
    gathered = gather(prolong[0])
    staged = products(a_blocks[0], col_index[0], prolong[0], gathered, target[0])
    return scatter(staged)


def solution(mesh):
    return jax.shard_map(
        shards,
        mesh=mesh,
        in_specs=(
            P("grp", "blk", None, None, None),
            P("grp", "blk", None),
            P("grp", "blk", None, None, None),
            P("grp", "blk", None),
        ),
        out_specs=P("grp", "blk", None, None),
        check_vma=False,
    )
```

```python
import functools

import jax
import jax.numpy as jnp
from jax import lax
from jax.experimental import pallas as pl
from jax.experimental.pallas import tpu as pltpu
from jax.sharding import PartitionSpec as P

f32, bf16 = jnp.float32, jnp.bfloat16
MESH = pl.DeviceIdType.MESH

B = 96
LANES = 128
PACK = 72
KP = 2
KA = 27
FR = 24
MEMBERS = 8
GROUPS = 16
OWN = 4
SLOTS = 512
PARTS = 6
PIECE = OWN * PACK // PARTS
STEPS = 6
WIDE_FROM = 2

BITS = ("xg", "yg", "zg", "xh", "yh", "zh")


def bits_of(grp, blk):
    x, zl = blk % 4, blk // 4
    y, zh, core = grp // 4, (grp // 2) % 2, grp % 2
    xh, yh = x // 2, y // 2
    return {
        "xg": (xh + x % 2) % 2, "yg": (yh + y % 2) % 2, "zg": (zh + zl) % 2,
        "xh": xh, "yh": yh, "zh": zh, "core": core,
    }


def partner_of(grp, blk, bit):
    x, zl = blk % 4, blk // 4
    y, zh, core = grp // 4, (grp // 2) % 2, grp % 2
    if bit == "xg":
        x = x + 1 - 2 * (x % 2)
    elif bit == "xh":
        x = 3 - x
    elif bit == "yg":
        y = y + 1 - 2 * (y % 2)
    elif bit == "yh":
        y = 3 - y
    elif bit in ("zg", "zl"):
        zl = 1 - zl
    elif bit == "zh":
        zl, zh = 1 - zl, 1 - zh
    elif bit == "core":
        core = 1 - core
    return {"blk": zl * 4 + x, "grp": y * 4 + zh * 2 + core}


def order_of(part):
    return [BITS[(part + step) % STEPS] for step in range(STEPS)]


def slot_of(target):
    owner = target // OWN
    bits = bits_of(owner // MEMBERS, owner % MEMBERS)
    index = bits["core"]
    for bit in BITS:
        index = index * 2 + bits[bit]
    return index * OWN + target % OWN


def enter(partners):
    barrier = pltpu.get_barrier_semaphore()
    for device in partners:
        pl.semaphore_signal(barrier, inc=1, device_id=device, device_id_type=MESH)
    pl.semaphore_wait(barrier, len(partners))


def fold(main, tail):
    lane = lax.broadcasted_iota(jnp.int32, main.shape, 1)
    side = jnp.concatenate([pltpu.roll(tail, shift, 1) for shift in (96, 64, 32)], axis=0)
    return jnp.where(lane < B, main, side)


def unfold(packed):
    n = packed.shape[0] // 3
    lane = lax.broadcasted_iota(jnp.int32, (n, LANES), 1)
    first = pltpu.roll(packed[:n], 32, 1)
    second = pltpu.roll(packed[n:2 * n], 64, 1)
    third = pltpu.roll(packed[2 * n:], 96, 1)
    return jnp.where(lane < 32, first, jnp.where(lane < 64, second, third))


G_ORDERS = (("xg", "xh", "zl"), ("xh", "zl", "xg"), ("zl", "xg", "xh"))
G_PARTS = 3
G_ROWS = FR // G_PARTS


def member(part, blk, flip):
    x, zl = blk % 4, blk // 4
    xh = x // 2
    bits = {"xg": (xh + x % 2) % 2, "xh": xh, "zl": zl}
    index = 0
    for i, bit in enumerate(G_ORDERS[part]):
        if flip >> i & 1:
            bits[bit] = 1 - bits[bit]
        index = index + bits[bit] * (1 << i)
    return index, bits["zl"] * 4 + bits["xh"] * 2 + (bits["xh"] + bits["xg"]) % 2


def gather_kernel(p_ref, out_ref, landed, send_sem, recv_sem):
    grp, blk = lax.axis_index("grp"), lax.axis_index("blk")
    partners = {bit: partner_of(grp, blk, bit) for bit in G_ORDERS[0]}
    where = [[member(part, blk, flip) for flip in range(MEMBERS)] for part in range(G_PARTS)]
    for part in range(G_PARTS):
        mine = where[part][0][0]

        def pack(r, _):
            v = p_ref[part * G_ROWS + r].astype(f32)
            v = jnp.pad(v.reshape(KP * B, B), ((0, 0), (0, LANES - B)))
            landed[part, mine, r] = fold(v[:KP * PACK], v[KP * PACK:]).astype(bf16)
            return 0
        lax.fori_loop(0, G_ROWS, pack, 0, unroll=True)
    enter(list(partners.values()))
    sends = []
    arrivals = {}

    def forward(part, flip, step):
        index = where[part][flip][0]
        copy = pltpu.make_async_remote_copy(
            src_ref=landed.at[part, index], dst_ref=landed.at[part, index],
            send_sem=send_sem.at[part, (1 << step) - 1 + flip], recv_sem=recv_sem.at[part, (1 << step) + flip],
            device_id=partners[G_ORDERS[part][step]], device_id_type=MESH)
        copy.start()
        sends.append(copy)
        arrivals[part, (1 << step) + flip] = copy

    def unpack(part, flip):
        index, source = where[part][flip]

        def one(r, _):
            packed = landed[part, index, r]
            both = jnp.concatenate([packed, unfold(packed)], axis=0)
            row = source * FR + part * G_ROWS + r
            for n in range(KP):
                out_ref[row, :, n * LANES:(n + 1) * LANES] = both[n * B:(n + 1) * B]
            return 0
        lax.fori_loop(0, G_ROWS, one, 0, unroll=True)

    for step in range(3):
        for part in range(G_PARTS):
            forward(part, 0, step)
    for part in range(G_PARTS):
        unpack(part, 0)
    for flip in range(1, MEMBERS):
        for part in range(G_PARTS):
            arrivals[part, flip].wait_recv()
            for step in range(flip.bit_length(), 3):
                forward(part, flip, step)
        for part in range(G_PARTS):
            unpack(part, flip)
    for copy in sends:
        copy.wait_send()


def gather(prolong):
    return pl.pallas_call(
        gather_kernel,
        out_shape=jax.ShapeDtypeStruct((FR * MEMBERS, B, KP * LANES), bf16),
        in_specs=[pl.BlockSpec(memory_space=pltpu.VMEM)],
        out_specs=pl.BlockSpec(memory_space=pltpu.VMEM),
        scratch_shapes=[
            pltpu.VMEM((G_PARTS, MEMBERS, G_ROWS, KP * PACK, LANES), bf16),
            pltpu.SemaphoreType.DMA((G_PARTS, MEMBERS)), pltpu.SemaphoreType.DMA((G_PARTS, MEMBERS))],
        compiler_params=pltpu.CompilerParams(collective_id=0, has_side_effects=True, vmem_limit_bytes=20 << 20),
        name="gather_prolong",
    )(prolong)


A_SLOTS = 3


def product_kernel(col, tgt, a_ref, p_ref, chosen, acc, a_buf, p_trans, a_sem):
    def fetch(i):
        slot = i % A_SLOTS
        return pltpu.make_async_copy(a_ref.at[i], a_buf.at[slot], a_sem.at[slot])

    for i in range(A_SLOTS - 1):
        fetch(i).start()

    @pl.loop(0, SLOTS // 8)
    def _(s):
        for j in range(8):
            acc[s * 8 + j] = jnp.zeros((B, LANES), f32)

    @pl.loop(0, FR)
    def _(i):
        for n in range(KP):
            p_trans[n * B:(n + 1) * B, :] = p_ref[i, n].T
        pt = p_trans[...]
        fetch(i).wait()

        @pl.when(i + A_SLOTS - 1 < FR)
        def _():
            fetch(i + A_SLOTS - 1).start()

        a = a_buf.at[i % A_SLOTS]
        aps = [jnp.dot(a[k], chosen[col[i * KA + k]], preferred_element_type=f32).astype(bf16) for k in range(KA)]
        values = [jnp.dot(pt, ap, preferred_element_type=f32) for ap in aps]
        for k, value in enumerate(values):
            for n in range(KP):
                for m in range(KP):
                    slot = tgt[i * (KP * KA * KP) + n * (KA * KP) + k * KP + m]
                    acc[slot] += value[n * B:(n + 1) * B, m * LANES:(m + 1) * LANES]


def products(a_rows, columns, p_rows, chosen, slots):
    vmem = pl.BlockSpec(memory_space=pltpu.VMEM)
    smem = pl.BlockSpec(memory_space=pltpu.SMEM)
    return pl.pallas_call(
        product_kernel,
        out_shape=pltpu.VMEM((SLOTS, B, LANES), f32),
        in_specs=[smem, smem, pl.BlockSpec(memory_space=pl.ANY), vmem, vmem],
        out_specs=vmem,
        scratch_shapes=[
            pltpu.VMEM((A_SLOTS, KA, B, B), bf16),
            pltpu.VMEM((KP * B, B), bf16),
            pltpu.SemaphoreType.DMA((A_SLOTS,))],
        compiler_params=pltpu.CompilerParams(vmem_limit_bytes=8 << 20),
        name="products",
    )(columns.reshape(-1), slots.reshape(-1), a_rows, p_rows, chosen)


def wire(step):
    return f32 if step >= WIDE_FROM else bf16


def scatter_kernel(acc, out_ref, *refs):
    refs = list(refs)
    cross, other = refs.pop(0), refs.pop(0)
    keep = [refs.pop(0) for _ in range(STEPS)]
    give = [refs.pop(0) for _ in range(STEPS)]
    got = [refs.pop(0) for _ in range(STEPS)]
    core_send, core_recv, send_sem, recv_sem = refs
    grp, blk = lax.axis_index("grp"), lax.axis_index("blk")
    bits = bits_of(grp, blk)
    partners = {bit: partner_of(grp, blk, bit) for bit in BITS + ("core",)}
    core = bits["core"]
    lane = lax.broadcasted_iota(jnp.int32, (24, LANES), 1)

    def packed(part, side, entry):
        owner = side * 64 + entry % (1 << part) * (1 << (STEPS - part)) + entry // (1 << part)
        units = []
        for unit in (2 * (part % 3), 2 * (part % 3) + 1):
            j, u = part // 3 * 2 + unit // 3, unit % 3
            main = acc[owner * OWN + j, 24 * u:24 * u + 24]
            tail = acc[owner * OWN + j, PACK:]
            units.append(jnp.where(lane < B, main, pltpu.roll(tail, 96 - 32 * u, 1)))
        return jnp.concatenate(units, axis=0)

    enter(list(partners.values()))
    crossed = []
    for part in range(PARTS):
        def pack(e, _):
            cross[part, e] = packed(part, 1 - core, e).astype(bf16)
            return 0
        lax.fori_loop(0, 64, pack, 0, unroll=4)
        copy = pltpu.make_async_remote_copy(
            src_ref=cross.at[part], dst_ref=other.at[part],
            send_sem=core_send.at[part], recv_sem=core_recv.at[part],
            device_id=partners["core"], device_id_type=MESH)
        copy.start()
        crossed.append(copy)
    sends = [[None] * PARTS for _ in range(STEPS)]
    for step in range(STEPS):
        half = 32 >> step
        for part in range(PARTS):
            bit = order_of(part)[step]
            away, here = (1 - bits[bit]) * half, bits[bit] * half
            if step == 0:
                crossed[part].wait_recv()
            else:
                sends[step - 1][part].wait_recv()

            def combine(offset, target, dtype):
                def one(e, _):
                    if step == 0:
                        total = packed(part, core, offset + e) + other[part, offset + e].astype(f32)
                    else:
                        total = keep[step - 1][part, offset + e] + got[step - 1][part, offset + e].astype(f32)
                    target[part, e] = total.astype(dtype)
                    return 0
                lax.fori_loop(0, half, one, 0, unroll=min(half, 4))

            combine(away, give[step], wire(step))
            copy = pltpu.make_async_remote_copy(
                src_ref=give[step].at[part], dst_ref=got[step].at[part],
                send_sem=send_sem.at[step, part], recv_sem=recv_sem.at[step, part],
                device_id=partners[bit], device_id_type=MESH)
            copy.start()
            sends[step][part] = copy
            combine(here, keep[step], f32)
    pieces = []
    for part in range(PARTS):
        sends[-1][part].wait_recv()
        pieces.append(keep[-1][part, 0] + got[-1][part, 0])
    for pair in range(2):
        both = jnp.concatenate(pieces[pair * 3:pair * 3 + 3], axis=0)
        for j in range(2):
            block = both[j * PACK:(j + 1) * PACK]
            out_ref[0, pair * 2 + j, :PACK] = block[:, :B]
            out_ref[0, pair * 2 + j, PACK:] = unfold(block)[:, :B]
    for copy in crossed:
        copy.wait_send()
    for row in sends:
        for copy in row:
            copy.wait_send()


def scatter(acc):
    halves = [32 >> step for step in range(STEPS)]
    return pl.pallas_call(
        scatter_kernel,
        out_shape=jax.ShapeDtypeStruct((1, OWN, B, B), f32),
        in_specs=[pl.BlockSpec(memory_space=pltpu.VMEM)],
        out_specs=pl.BlockSpec(memory_space=pltpu.VMEM),
        scratch_shapes=(
            [pltpu.VMEM((PARTS, 64, PIECE, LANES), bf16)] * 2
            + [pltpu.VMEM((PARTS, n, PIECE, LANES), f32) for n in halves]
            + [pltpu.VMEM((PARTS, n, PIECE, LANES), wire(s)) for s, n in enumerate(halves)] * 2
            + [pltpu.SemaphoreType.DMA((PARTS,))] * 2
            + [pltpu.SemaphoreType.DMA((STEPS, PARTS))] * 2),
        compiler_params=pltpu.CompilerParams(collective_id=1, has_side_effects=True, vmem_limit_bytes=34 << 20),
        name="sum_at_owners",
    )(pltpu.with_memory_space_constraint(acc, pltpu.VMEM))


def shards(a_blocks, col_index, prolong, target):
    chosen = gather(prolong[0])
    acc = products(a_blocks[0], col_index[0], prolong[0], chosen, slot_of(target[0]))
    return scatter(acc)


def solution(mesh):
    return jax.shard_map(
        shards,
        mesh=mesh,
        in_specs=(
            P("grp", "blk", None, None, None),
            P("grp", "blk", None),
            P("grp", "blk", None, None, None),
            P("grp", "blk", None),
        ),
        out_specs=P("grp", "blk", None, None),
        check_vma=False,
    )
```

```python
import functools

import jax
import jax.numpy as jnp
from jax import lax
from jax.experimental import pallas as pl
from jax.experimental.pallas import tpu as pltpu
from jax.sharding import PartitionSpec as P

f32, bf16 = jnp.float32, jnp.bfloat16
MESH = pl.DeviceIdType.MESH

B = 96
LANES = 128
PACK = 72
KP = 2
KA = 27
FR = 24
MEMBERS = 8
GROUPS = 16
OWN = 4
SLOTS = 512
PARTS = 6
PIECE = OWN * PACK // PARTS
STEPS = 6

BITS = ("xg", "yg", "zg", "xh", "yh", "zh")


def bits_of(grp, blk):
    x, zl = blk % 4, blk // 4
    y, zh, core = grp // 4, (grp // 2) % 2, grp % 2
    xh, yh = x // 2, y // 2
    return {
        "xg": (xh + x % 2) % 2, "yg": (yh + y % 2) % 2, "zg": (zh + zl) % 2,
        "xh": xh, "yh": yh, "zh": zh, "core": core,
    }


def partner_of(grp, blk, bit):
    x, zl = blk % 4, blk // 4
    y, zh, core = grp // 4, (grp // 2) % 2, grp % 2
    if bit == "xg":
        x = x + 1 - 2 * (x % 2)
    elif bit == "xh":
        x = 3 - x
    elif bit == "yg":
        y = y + 1 - 2 * (y % 2)
    elif bit == "yh":
        y = 3 - y
    elif bit in ("zg", "zl"):
        zl = 1 - zl
    elif bit == "zh":
        zl, zh = 1 - zl, 1 - zh
    elif bit == "core":
        core = 1 - core
    return {"blk": zl * 4 + x, "grp": y * 4 + zh * 2 + core}


def order_of(part):
    return [BITS[(part + step) % STEPS] for step in range(STEPS)]


def slot_of(target):
    owner = target // OWN
    bits = bits_of(owner // MEMBERS, owner % MEMBERS)
    index = bits["core"]
    for bit in BITS:
        index = index * 2 + bits[bit]
    return index * OWN + target % OWN


def enter(partners):
    barrier = pltpu.get_barrier_semaphore()
    for device in partners:
        pl.semaphore_signal(barrier, inc=1, device_id=device, device_id_type=MESH)
    pl.semaphore_wait(barrier, len(partners))


def fold(main, tail):
    lane = lax.broadcasted_iota(jnp.int32, main.shape, 1)
    side = jnp.concatenate([pltpu.roll(tail, shift, 1) for shift in (96, 64, 32)], axis=0)
    return jnp.where(lane < B, main, side)


def unfold(packed):
    n = packed.shape[0] // 3
    lane = lax.broadcasted_iota(jnp.int32, (n, LANES), 1)
    first = pltpu.roll(packed[:n], 32, 1)
    second = pltpu.roll(packed[n:2 * n], 64, 1)
    third = pltpu.roll(packed[2 * n:], 96, 1)
    return jnp.where(lane < 32, first, jnp.where(lane < 64, second, third))


G_ORDERS = (("xg", "xh", "zl"), ("xh", "zl", "xg"), ("zl", "xg", "xh"))
G_PARTS = 3
G_ROWS = FR // G_PARTS


def member(part, blk, flip):
    x, zl = blk % 4, blk // 4
    xh = x // 2
    bits = {"xg": (xh + x % 2) % 2, "xh": xh, "zl": zl}
    index = 0
    for i, bit in enumerate(G_ORDERS[part]):
        if flip >> i & 1:
            bits[bit] = 1 - bits[bit]
        index = index + bits[bit] * (1 << i)
    return index, bits["zl"] * 4 + bits["xh"] * 2 + (bits["xh"] + bits["xg"]) % 2


def gather_kernel(p_ref, out_ref, landed, send_sem, recv_sem):
    grp, blk = lax.axis_index("grp"), lax.axis_index("blk")
    partners = {bit: partner_of(grp, blk, bit) for bit in G_ORDERS[0]}
    where = [[member(part, blk, flip) for flip in range(MEMBERS)] for part in range(G_PARTS)]
    for part in range(G_PARTS):
        mine = where[part][0][0]

        def pack(r, _):
            v = p_ref[part * G_ROWS + r].astype(f32)
            v = jnp.pad(v.reshape(KP * B, B), ((0, 0), (0, LANES - B)))
            landed[part, mine, r] = fold(v[:KP * PACK], v[KP * PACK:]).astype(bf16)
            return 0
        lax.fori_loop(0, G_ROWS, pack, 0, unroll=True)
    enter(list(partners.values()))
    sends = []
    arrivals = {}

    def forward(part, flip, step):
        index = where[part][flip][0]
        copy = pltpu.make_async_remote_copy(
            src_ref=landed.at[part, index], dst_ref=landed.at[part, index],
            send_sem=send_sem.at[part, (1 << step) - 1 + flip], recv_sem=recv_sem.at[part, (1 << step) + flip],
            device_id=partners[G_ORDERS[part][step]], device_id_type=MESH)
        copy.start()
        sends.append(copy)
        arrivals[part, (1 << step) + flip] = copy

    def unpack(part, flip):
        index, source = where[part][flip]

        def one(r, _):
            packed = landed[part, index, r]
            both = jnp.concatenate([packed, unfold(packed)], axis=0)
            row = source * FR + part * G_ROWS + r
            for n in range(KP):
                out_ref[row, :, n * LANES:(n + 1) * LANES] = both[n * B:(n + 1) * B]
            return 0
        lax.fori_loop(0, G_ROWS, one, 0, unroll=True)

    for step in range(3):
        for part in range(G_PARTS):
            forward(part, 0, step)
    for part in range(G_PARTS):
        unpack(part, 0)
    for flip in range(1, MEMBERS):
        for part in range(G_PARTS):
            arrivals[part, flip].wait_recv()
            for step in range(flip.bit_length(), 3):
                forward(part, flip, step)
        for part in range(G_PARTS):
            unpack(part, flip)
    for copy in sends:
        copy.wait_send()


def gather(prolong):
    return pl.pallas_call(
        gather_kernel,
        out_shape=jax.ShapeDtypeStruct((FR * MEMBERS, B, KP * LANES), bf16),
        in_specs=[pl.BlockSpec(memory_space=pltpu.VMEM)],
        out_specs=pl.BlockSpec(memory_space=pltpu.VMEM),
        scratch_shapes=[
            pltpu.VMEM((G_PARTS, MEMBERS, G_ROWS, KP * PACK, LANES), bf16),
            pltpu.SemaphoreType.DMA((G_PARTS, MEMBERS)), pltpu.SemaphoreType.DMA((G_PARTS, MEMBERS))],
        compiler_params=pltpu.CompilerParams(collective_id=0, has_side_effects=True, vmem_limit_bytes=20 << 20),
        name="gather_prolong",
    )(prolong)


A_SLOTS = 3
AHEAD = 8


def product_kernel(col, tgt, a_ref, p_ref, chosen, acc, a_buf, p_trans, a_sem):
    def fetch(i):
        slot = i % A_SLOTS
        return pltpu.make_async_copy(a_ref.at[i], a_buf.at[slot], a_sem.at[slot])

    for i in range(A_SLOTS - 1):
        fetch(i).start()

    @pl.loop(0, SLOTS // 8)
    def _(s):
        for j in range(8):
            acc[s * 8 + j] = jnp.zeros((B, LANES), f32)

    @pl.loop(0, FR)
    def _(i):
        for n in range(KP):
            p_trans[n * B:(n + 1) * B, :] = p_ref[i, n].T
        pt = p_trans[...]
        fetch(i).wait()

        @pl.when(i + A_SLOTS - 1 < FR)
        def _():
            fetch(i + A_SLOTS - 1).start()

        a = a_buf.at[i % A_SLOTS]
        aps, values = {}, {}
        for u in range(KA + 2 * AHEAD):
            if u < KA:
                aps[u] = jnp.dot(a[u], chosen[col[i * KA + u]], preferred_element_type=f32).astype(bf16)
            if 0 <= u - AHEAD < KA:
                values[u - AHEAD] = jnp.dot(pt, aps.pop(u - AHEAD), preferred_element_type=f32)
            k = u - 2 * AHEAD
            if k < 0:
                continue
            value = values.pop(k)
            for n in range(KP):
                for m in range(KP):
                    slot = tgt[i * (KP * KA * KP) + n * (KA * KP) + k * KP + m]
                    acc[slot] += value[n * B:(n + 1) * B, m * LANES:(m + 1) * LANES]


def products(a_rows, columns, p_rows, chosen, slots):
    vmem = pl.BlockSpec(memory_space=pltpu.VMEM)
    smem = pl.BlockSpec(memory_space=pltpu.SMEM)
    return pl.pallas_call(
        product_kernel,
        out_shape=pltpu.VMEM((SLOTS, B, LANES), f32),
        in_specs=[smem, smem, pl.BlockSpec(memory_space=pl.ANY), vmem, vmem],
        out_specs=vmem,
        scratch_shapes=[
            pltpu.VMEM((A_SLOTS, KA, B, B), bf16),
            pltpu.VMEM((KP * B, B), bf16),
            pltpu.SemaphoreType.DMA((A_SLOTS,))],
        compiler_params=pltpu.CompilerParams(vmem_limit_bytes=8 << 20),
        name="products",
    )(columns.reshape(-1), slots.reshape(-1), a_rows, p_rows, chosen)


def flipped(grp, blk, flips):
    place = {"grp": grp, "blk": blk}
    for bit in flips:
        place = partner_of(place["grp"], place["blk"], bit)
    return place


def direct(part, relative):
    return [bit for i, bit in enumerate(order_of(part)[3:]) if relative >> (2 - i) & 1]


def scatter_kernel(acc, out_ref, cross, other, keep0, give0, got0, keep1, give1, got1, keep2, give2, got2, last, arrived, total,
                   core_send, core_recv, send0, recv0, send1, recv1, send2, recv2, last_send, last_recv):
    grp, blk = lax.axis_index("grp"), lax.axis_index("blk")
    bits = bits_of(grp, blk)
    core = bits["core"]
    mine = [[bits[bit] for bit in order_of(part)] for part in range(PARTS)]
    lane = lax.broadcasted_iota(jnp.int32, (24, LANES), 1)
    flips = sorted({tuple(sorted(direct(part, r))) for part in range(PARTS) for r in range(1, 8)}) + [("core",)]
    partners = {f: flipped(grp, blk, f) for f in flips}

    def packed(part, side, entry):
        owner = side * 64 + entry % (1 << part) * (1 << (STEPS - part)) + entry // (1 << part)
        units = []
        for unit in (2 * (part % 3), 2 * (part % 3) + 1):
            j, u = part // 3 * 2 + unit // 3, unit % 3
            main = acc[owner * OWN + j, 24 * u:24 * u + 24]
            tail = acc[owner * OWN + j, PACK:]
            units.append(jnp.where(lane < B, main, pltpu.roll(tail, 96 - 32 * u, 1)))
        return jnp.concatenate(units, axis=0)

    def fill(target, n, value):
        def one(e, _):
            target[e] = value(e).astype(target.dtype)
            return 0
        lax.fori_loop(0, n, one, 0, unroll=4)

    started = []

    def send(source, target, send_sem, recv_sem, device):
        copy = pltpu.make_async_remote_copy(
            src_ref=source, dst_ref=target, send_sem=send_sem, recv_sem=recv_sem,
            device_id=device, device_id_type=MESH)
        copy.start()
        started.append(copy)
        return copy

    barrier = pltpu.get_barrier_semaphore()
    for device in partners.values():
        pl.semaphore_signal(barrier, inc=1, device_id=device, device_id_type=MESH)

    crossed, first, second, third, final = {}, {}, {}, {}, {}
    for chunk in range(2):
        for part in range(PARTS):
            offset = (1 - mine[part][0] if chunk == 0 else mine[part][0]) * 32
            fill(cross.at[part, chunk], 32, lambda e: packed(part, 1 - core, offset + e))
            if chunk == 0 and part == 0:
                pl.semaphore_wait(barrier, len(flips))
            crossed[part, chunk] = send(
                cross.at[part, chunk], other.at[part, chunk], core_send.at[part, chunk], core_recv.at[part, chunk],
                partners[("core",)])

    for part in range(PARTS):
        crossed[part, 0].wait_recv()
        for chunk in range(2):
            offset = (1 - mine[part][1] if chunk == 0 else mine[part][1]) * 16
            away = (1 - mine[part][0]) * 32 + offset
            fill(give0.at[part, chunk], 16,
                 lambda e: packed(part, core, away + e) + other[part, 0, offset + e].astype(f32))
            first[part, chunk] = send(
                give0.at[part, chunk], got0.at[part, chunk], send0.at[part, chunk], recv0.at[part, chunk],
                partners[(order_of(part)[0],)])
    for part in range(PARTS):
        crossed[part, 1].wait_recv()
        for chunk in range(2):
            offset = (1 - mine[part][1] if chunk == 0 else mine[part][1]) * 16
            here = mine[part][0] * 32 + offset
            fill(keep0.at[part, chunk], 16,
                 lambda e: packed(part, core, here + e) + other[part, 1, offset + e].astype(f32))

    for part in range(PARTS):
        first[part, 0].wait_recv()
        for chunk in range(2):
            offset = (1 - mine[part][2] if chunk == 0 else mine[part][2]) * 8
            fill(give1.at[part, chunk], 8,
                 lambda e: keep0[part, 0, offset + e] + got0[part, 0, offset + e].astype(f32))
            second[part, chunk] = send(
                give1.at[part, chunk], got1.at[part, chunk], send1.at[part, chunk], recv1.at[part, chunk],
                partners[(order_of(part)[1],)])
    for part in range(PARTS):
        first[part, 1].wait_recv()
        for chunk in range(2):
            offset = (1 - mine[part][2] if chunk == 0 else mine[part][2]) * 8
            fill(keep1.at[part, chunk], 8,
                 lambda e: keep0[part, 1, offset + e] + got0[part, 1, offset + e].astype(f32))

    for part in range(PARTS):
        second[part, 0].wait_recv()
        fill(give2.at[part], 8, lambda e: keep1[part, 0, e] + got1[part, 0, e].astype(f32))
        third[part] = send(
            give2.at[part], got2.at[part], send2.at[part], recv2.at[part], partners[(order_of(part)[2],)])
    for part in range(PARTS):
        second[part, 1].wait_recv()
        fill(keep2.at[part], 8, lambda e: keep1[part, 1, e] + got1[part, 1, e].astype(f32))

    for part in range(PARTS):
        third[part].wait_recv()
        for r in range(8):
            entry = 0
            for i in range(3):
                bit = mine[part][3 + i]
                entry = entry * 2 + (1 - bit if r >> (2 - i) & 1 else bit)
            value = keep2[part, entry] + got2[part, entry].astype(f32)
            if r == 0:
                total[part] = value
                continue
            last[part, r - 1] = value.astype(bf16)
            final[part, r] = send(
                last.at[part, r - 1], arrived.at[part, r - 1], last_send.at[part, r - 1], last_recv.at[part, r - 1],
                partners[tuple(sorted(direct(part, r)))])
    pieces = []
    for part in range(PARTS):
        value = total[part]
        for r in range(1, 8):
            final[part, r].wait_recv()
            value = value + arrived[part, r - 1].astype(f32)
        pieces.append(value)
    for pair in range(2):
        both = jnp.concatenate(pieces[pair * 3:pair * 3 + 3], axis=0)
        for j in range(2):
            block = both[j * PACK:(j + 1) * PACK]
            out_ref[0, pair * 2 + j, :PACK] = block[:, :B]
            out_ref[0, pair * 2 + j, PACK:] = unfold(block)[:, :B]
    for copy in started:
        copy.wait_send()


def scatter(acc):
    def piece(dtype, *lead):
        return pltpu.VMEM((PARTS,) + lead + (PIECE, LANES), dtype)
    dma = pltpu.SemaphoreType.DMA
    return pl.pallas_call(
        scatter_kernel,
        out_shape=jax.ShapeDtypeStruct((1, OWN, B, B), f32),
        in_specs=[pl.BlockSpec(memory_space=pltpu.VMEM)],
        out_specs=pl.BlockSpec(memory_space=pltpu.VMEM),
        scratch_shapes=[
            piece(bf16, 2, 32), piece(bf16, 2, 32),
            piece(f32, 2, 16), piece(bf16, 2, 16), piece(bf16, 2, 16),
            piece(f32, 2, 8), piece(bf16, 2, 8), piece(bf16, 2, 8),
            piece(f32, 8), piece(bf16, 8), piece(bf16, 8),
            piece(bf16, 7), piece(bf16, 7), piece(f32)]
            + [dma((PARTS, 2))] * 6 + [dma((PARTS,))] * 2 + [dma((PARTS, 7))] * 2,
        compiler_params=pltpu.CompilerParams(collective_id=1, has_side_effects=True, vmem_limit_bytes=30 << 20),
        name="sum_at_owners",
    )(pltpu.with_memory_space_constraint(acc, pltpu.VMEM))


def shards(a_blocks, col_index, prolong, target):
    chosen = gather(prolong[0])
    acc = products(a_blocks[0], col_index[0], prolong[0], chosen, slot_of(target[0]))
    return scatter(acc)


def solution(mesh):
    return jax.shard_map(
        shards,
        mesh=mesh,
        in_specs=(
            P("grp", "blk", None, None, None),
            P("grp", "blk", None),
            P("grp", "blk", None, None, None),
            P("grp", "blk", None),
        ),
        out_specs=P("grp", "blk", None, None),
        check_vma=False,
    )
```

```python
import functools

import jax
import jax.numpy as jnp
from jax import lax
from jax.experimental import pallas as pl
from jax.experimental.pallas import tpu as pltpu
from jax.sharding import PartitionSpec as P

f32, bf16 = jnp.float32, jnp.bfloat16
MESH = pl.DeviceIdType.MESH

B = 96
LANES = 128
PACK = 72
KP = 2
KA = 27
FR = 24
MEMBERS = 8
GROUPS = 16
OWN = 4
SLOTS = 512
PARTS = 6
PIECE = OWN * PACK // PARTS
STEPS = 6

BITS = ("xg", "yg", "zg", "xh", "yh", "zh")


def bits_of(grp, blk):
    x, zl = blk % 4, blk // 4
    y, zh, core = grp // 4, (grp // 2) % 2, grp % 2
    xh, yh = x // 2, y // 2
    return {
        "xg": (xh + x % 2) % 2, "yg": (yh + y % 2) % 2, "zg": (zh + zl) % 2,
        "xh": xh, "yh": yh, "zh": zh, "core": core,
    }


def partner_of(grp, blk, bit):
    x, zl = blk % 4, blk // 4
    y, zh, core = grp // 4, (grp // 2) % 2, grp % 2
    if bit == "xg":
        x = x + 1 - 2 * (x % 2)
    elif bit == "xh":
        x = 3 - x
    elif bit == "yg":
        y = y + 1 - 2 * (y % 2)
    elif bit == "yh":
        y = 3 - y
    elif bit in ("zg", "zl"):
        zl = 1 - zl
    elif bit == "zh":
        zl, zh = 1 - zl, 1 - zh
    elif bit == "core":
        core = 1 - core
    return {"blk": zl * 4 + x, "grp": y * 4 + zh * 2 + core}


def order_of(part):
    return [BITS[(part + step) % STEPS] for step in range(STEPS)]


def slot_of(target):
    owner = target // OWN
    bits = bits_of(owner // MEMBERS, owner % MEMBERS)
    index = bits["core"]
    for bit in BITS:
        index = index * 2 + bits[bit]
    return index * OWN + target % OWN


def fold(main, tail):
    lane = lax.broadcasted_iota(jnp.int32, main.shape, 1)
    side = jnp.concatenate([pltpu.roll(tail, shift, 1) for shift in (96, 64, 32)], axis=0)
    return jnp.where(lane < B, main, side)


def unfold(packed):
    n = packed.shape[0] // 3
    lane = lax.broadcasted_iota(jnp.int32, (n, LANES), 1)
    first = pltpu.roll(packed[:n], 32, 1)
    second = pltpu.roll(packed[n:2 * n], 64, 1)
    third = pltpu.roll(packed[2 * n:], 96, 1)
    return jnp.where(lane < 32, first, jnp.where(lane < 64, second, third))


G_ORDERS = (("xg", "xh", "zl"), ("xh", "zl", "xg"), ("zl", "xg", "xh"))
G_PARTS = 3
G_ROWS = FR // G_PARTS
G_BATCH = 4


def member(part, blk, flip):
    x, zl = blk % 4, blk // 4
    xh = x // 2
    bits = {"xg": (xh + x % 2) % 2, "xh": xh, "zl": zl}
    index = 0
    for i, bit in enumerate(G_ORDERS[part]):
        if flip >> i & 1:
            bits[bit] = 1 - bits[bit]
        index = index + bits[bit] * (1 << i)
    return index, bits["zl"] * 4 + bits["xh"] * 2 + (bits["xh"] + bits["xg"]) % 2


def gather_kernel(p_ref, out_ref, landed, send_sem, recv_sem):
    grp, blk = lax.axis_index("grp"), lax.axis_index("blk")
    partners = {bit: partner_of(grp, blk, bit) for bit in G_ORDERS[0]}
    barrier = pltpu.get_barrier_semaphore()
    for device in partners.values():
        pl.semaphore_signal(barrier, inc=1, device_id=device, device_id_type=MESH)
    where = [[member(part, blk, flip) for flip in range(MEMBERS)] for part in range(G_PARTS)]
    for part in range(G_PARTS):
        mine = where[part][0][0]

        for low in range(0, G_ROWS, G_BATCH):
            packed = []
            for r in range(low, low + G_BATCH):
                v = p_ref[part * G_ROWS + r].reshape(KP * B, B)
                v = jnp.pad(v, ((0, 0), (0, LANES - B)))
                packed.append(fold(v[:KP * PACK], v[KP * PACK:]))
            for r in range(G_BATCH):
                landed[part, mine, low + r] = packed[r]
    pl.semaphore_wait(barrier, len(partners))
    sends = []
    arrivals = {}

    def forward(part, flip, step):
        index = where[part][flip][0]
        copy = pltpu.make_async_remote_copy(
            src_ref=landed.at[part, index], dst_ref=landed.at[part, index],
            send_sem=send_sem.at[part, (1 << step) - 1 + flip], recv_sem=recv_sem.at[part, (1 << step) + flip],
            device_id=partners[G_ORDERS[part][step]], device_id_type=MESH)
        copy.start()
        sends.append(copy)
        arrivals[part, (1 << step) + flip] = copy

    def unpack(part, flip):
        index, source = where[part][flip]

        row = source * FR + part * G_ROWS
        for low in range(0, G_ROWS, G_BATCH):
            packed = [landed[part, index, low + r] for r in range(G_BATCH)]
            tails = [unfold(v) for v in packed]
            for r in range(G_BATCH):
                both = jnp.concatenate([packed[r], tails[r]], axis=0)
                for n in range(KP):
                    out_ref[row + low + r, :, n * LANES:(n + 1) * LANES] = both[n * B:(n + 1) * B]

    for step in range(3):
        for part in range(G_PARTS):
            forward(part, 0, step)
    for part in range(G_PARTS):
        unpack(part, 0)
    for flip in range(1, MEMBERS):
        for part in range(G_PARTS):
            arrivals[part, flip].wait_recv()
            for step in range(flip.bit_length(), 3):
                forward(part, flip, step)
        for part in range(G_PARTS):
            unpack(part, flip)
    for copy in sends:
        copy.wait_send()


def gather(prolong):
    return pl.pallas_call(
        gather_kernel,
        out_shape=jax.ShapeDtypeStruct((FR * MEMBERS, B, KP * LANES), bf16),
        in_specs=[pl.BlockSpec(memory_space=pltpu.VMEM)],
        out_specs=pl.BlockSpec(memory_space=pltpu.VMEM),
        scratch_shapes=[
            pltpu.VMEM((G_PARTS, MEMBERS, G_ROWS, KP * PACK, LANES), bf16),
            pltpu.SemaphoreType.DMA((G_PARTS, MEMBERS)), pltpu.SemaphoreType.DMA((G_PARTS, MEMBERS))],
        compiler_params=pltpu.CompilerParams(collective_id=0, has_side_effects=True, vmem_limit_bytes=20 << 20),
        name="gather_prolong",
    )(prolong)


A_SLOTS = 3
AHEAD = 8


def product_kernel(col, tgt, a_ref, p_ref, chosen, acc, a_buf, p_trans, a_sem):
    def fetch(i):
        slot = i % A_SLOTS
        return pltpu.make_async_copy(a_ref.at[i], a_buf.at[slot], a_sem.at[slot])

    for i in range(A_SLOTS - 1):
        fetch(i).start()

    @pl.loop(0, SLOTS // 8)
    def _(s):
        for j in range(8):
            acc[s * 8 + j] = jnp.zeros((B, LANES), f32)

    @pl.loop(0, FR)
    def _(i):
        for n in range(KP):
            p_trans[n * B:(n + 1) * B, :] = p_ref[i, n].T
        pt = p_trans[...]
        fetch(i).wait()

        @pl.when(i + A_SLOTS - 1 < FR)
        def _():
            fetch(i + A_SLOTS - 1).start()

        a = a_buf.at[i % A_SLOTS]
        aps, values = {}, {}
        for u in range(KA + 2 * AHEAD):
            if u < KA:
                aps[u] = jnp.dot(a[u], chosen[col[i * KA + u]], preferred_element_type=f32).astype(bf16)
            if 0 <= u - AHEAD < KA:
                values[u - AHEAD] = jnp.dot(pt, aps.pop(u - AHEAD), preferred_element_type=f32)
            k = u - 2 * AHEAD
            if k < 0:
                continue
            value = values.pop(k)
            for n in range(KP):
                for m in range(KP):
                    slot = tgt[i * (KP * KA * KP) + n * (KA * KP) + k * KP + m]
                    acc[slot] += value[n * B:(n + 1) * B, m * LANES:(m + 1) * LANES]


def products(a_rows, columns, p_rows, chosen, slots):
    vmem = pl.BlockSpec(memory_space=pltpu.VMEM)
    smem = pl.BlockSpec(memory_space=pltpu.SMEM)
    return pl.pallas_call(
        product_kernel,
        out_shape=pltpu.VMEM((SLOTS, B, LANES), f32),
        in_specs=[smem, smem, pl.BlockSpec(memory_space=pl.ANY), vmem, vmem],
        out_specs=vmem,
        scratch_shapes=[
            pltpu.VMEM((A_SLOTS, KA, B, B), bf16),
            pltpu.VMEM((KP * B, B), bf16),
            pltpu.SemaphoreType.DMA((A_SLOTS,))],
        compiler_params=pltpu.CompilerParams(vmem_limit_bytes=8 << 20),
        name="products",
    )(columns.reshape(-1), slots.reshape(-1), a_rows, p_rows, chosen)


BATCH = 16


def flipped(grp, blk, flips):
    place = {"grp": grp, "blk": blk}
    for bit in flips:
        place = partner_of(place["grp"], place["blk"], bit)
    return place


def direct(part, relative):
    return [bit for i, bit in enumerate(order_of(part)[3:]) if relative >> (2 - i) & 1]


def scatter_kernel(acc, out_ref, cross, other, keep0, give0, got0, keep1, give1, got1, keep2, give2, got2, last, arrived, total,
                   core_send, core_recv, send0, recv0, send1, recv1, send2, recv2, last_send, last_recv):
    grp, blk = lax.axis_index("grp"), lax.axis_index("blk")
    bits = bits_of(grp, blk)
    core = bits["core"]
    mine = [[bits[bit] for bit in order_of(part)] for part in range(PARTS)]
    lane = lax.broadcasted_iota(jnp.int32, (24, LANES), 1)
    flips = sorted({tuple(sorted(direct(part, r))) for part in range(PARTS) for r in range(1, 8)}) + [("core",)]
    partners = {f: flipped(grp, blk, f) for f in flips}

    def packed(part, side, entry):
        owner = side * 64 + entry % (1 << part) * (1 << (STEPS - part)) + entry // (1 << part)
        units = []
        for unit in (2 * (part % 3), 2 * (part % 3) + 1):
            j, u = part // 3 * 2 + unit // 3, unit % 3
            main = acc[owner * OWN + j, 24 * u:24 * u + 24]
            tail = acc[owner * OWN + j, PACK:]
            units.append(jnp.where(lane < B, main, pltpu.roll(tail, 96 - 32 * u, 1)))
        return jnp.concatenate(units, axis=0)

    def fill(target, n, value):
        def some(g, _):
            values = [value(g * batch + e).astype(target.dtype) for e in range(batch)]
            for e in range(batch):
                target[g * batch + e] = values[e]
            return 0
        batch = min(n, BATCH)
        lax.fori_loop(0, n // batch, some, 0)

    started = []

    def send(source, target, send_sem, recv_sem, device):
        copy = pltpu.make_async_remote_copy(
            src_ref=source, dst_ref=target, send_sem=send_sem, recv_sem=recv_sem,
            device_id=device, device_id_type=MESH)
        copy.start()
        started.append(copy)
        return copy

    barrier = pltpu.get_barrier_semaphore()
    for device in partners.values():
        pl.semaphore_signal(barrier, inc=1, device_id=device, device_id_type=MESH)

    crossed, first, second, third, final = {}, {}, {}, {}, {}
    def cross_over(part, chunk):
        offset = (1 - mine[part][0] if chunk == 0 else mine[part][0]) * 32
        fill(cross.at[part, chunk], 32, lambda e: packed(part, 1 - core, offset + e))
        if chunk == 0 and part == 0:
            pl.semaphore_wait(barrier, len(flips))
        crossed[part, chunk] = send(
            cross.at[part, chunk], other.at[part, chunk], core_send.at[part, chunk], core_recv.at[part, chunk],
            partners[("core",)])

    def give_away(part):
        crossed[part, 0].wait_recv()
        for chunk in range(2):
            offset = (1 - mine[part][1] if chunk == 0 else mine[part][1]) * 16
            away = (1 - mine[part][0]) * 32 + offset
            fill(give0.at[part, chunk], 16,
                 lambda e: packed(part, core, away + e) + other[part, 0, offset + e].astype(f32))
            first[part, chunk] = send(
                give0.at[part, chunk], got0.at[part, chunk], send0.at[part, chunk], recv0.at[part, chunk],
                partners[(order_of(part)[0],)])

    cross_over(0, 0)
    cross_over(1, 0)
    for part in range(PARTS):
        if part + 2 < PARTS:
            cross_over(part + 2, 0)
        give_away(part)
    for part in range(PARTS):
        cross_over(part, 1)
    for part in range(PARTS):
        crossed[part, 1].wait_recv()
        for chunk in range(2):
            offset = (1 - mine[part][1] if chunk == 0 else mine[part][1]) * 16
            here = mine[part][0] * 32 + offset
            fill(keep0.at[part, chunk], 16,
                 lambda e: packed(part, core, here + e) + other[part, 1, offset + e].astype(f32))

    for part in range(PARTS):
        first[part, 0].wait_recv()
        for chunk in range(2):
            offset = (1 - mine[part][2] if chunk == 0 else mine[part][2]) * 8
            fill(give1.at[part, chunk], 8,
                 lambda e: keep0[part, 0, offset + e] + got0[part, 0, offset + e].astype(f32))
            second[part, chunk] = send(
                give1.at[part, chunk], got1.at[part, chunk], send1.at[part, chunk], recv1.at[part, chunk],
                partners[(order_of(part)[1],)])
    for part in range(PARTS):
        first[part, 1].wait_recv()
        for chunk in range(2):
            offset = (1 - mine[part][2] if chunk == 0 else mine[part][2]) * 8
            fill(keep1.at[part, chunk], 8,
                 lambda e: keep0[part, 1, offset + e] + got0[part, 1, offset + e].astype(f32))

    for part in range(PARTS):
        second[part, 0].wait_recv()
        fill(give2.at[part], 8, lambda e: keep1[part, 0, e] + got1[part, 0, e].astype(f32))
        third[part] = send(
            give2.at[part], got2.at[part], send2.at[part], recv2.at[part], partners[(order_of(part)[2],)])
    for part in range(PARTS):
        second[part, 1].wait_recv()
        fill(keep2.at[part], 8, lambda e: keep1[part, 1, e] + got1[part, 1, e].astype(f32))

    for part in range(PARTS):
        third[part].wait_recv()
        for r in range(8):
            entry = 0
            for i in range(3):
                bit = mine[part][3 + i]
                entry = entry * 2 + (1 - bit if r >> (2 - i) & 1 else bit)
            value = keep2[part, entry] + got2[part, entry].astype(f32)
            if r == 0:
                total[part] = value
                continue
            last[part, r - 1] = value.astype(bf16)
            final[part, r] = send(
                last.at[part, r - 1], arrived.at[part, r - 1], last_send.at[part, r - 1], last_recv.at[part, r - 1],
                partners[tuple(sorted(direct(part, r)))])
    pieces = []
    for part in range(PARTS):
        value = total[part]
        for r in range(1, 8):
            final[part, r].wait_recv()
            value = value + arrived[part, r - 1].astype(f32)
        pieces.append(value)
    for pair in range(2):
        both = jnp.concatenate(pieces[pair * 3:pair * 3 + 3], axis=0)
        for j in range(2):
            block = both[j * PACK:(j + 1) * PACK]
            out_ref[0, pair * 2 + j, :PACK] = block[:, :B]
            out_ref[0, pair * 2 + j, PACK:] = unfold(block)[:, :B]
    for copy in started:
        copy.wait_send()


def scatter(acc):
    def piece(dtype, *lead):
        return pltpu.VMEM((PARTS,) + lead + (PIECE, LANES), dtype)
    dma = pltpu.SemaphoreType.DMA
    return pl.pallas_call(
        scatter_kernel,
        out_shape=jax.ShapeDtypeStruct((1, OWN, B, B), f32),
        in_specs=[pl.BlockSpec(memory_space=pltpu.VMEM)],
        out_specs=pl.BlockSpec(memory_space=pltpu.VMEM),
        scratch_shapes=[
            piece(bf16, 2, 32), piece(bf16, 2, 32),
            piece(f32, 2, 16), piece(bf16, 2, 16), piece(bf16, 2, 16),
            piece(f32, 2, 8), piece(bf16, 2, 8), piece(bf16, 2, 8),
            piece(f32, 8), piece(bf16, 8), piece(bf16, 8),
            piece(bf16, 7), piece(bf16, 7), piece(f32)]
            + [dma((PARTS, 2))] * 6 + [dma((PARTS,))] * 2 + [dma((PARTS, 7))] * 2,
        compiler_params=pltpu.CompilerParams(collective_id=1, has_side_effects=True, vmem_limit_bytes=30 << 20),
        name="sum_at_owners",
    )(pltpu.with_memory_space_constraint(acc, pltpu.VMEM))


def shards(a_blocks, col_index, prolong, target):
    chosen = gather(prolong[0])
    acc = products(a_blocks[0], col_index[0], prolong[0], chosen, slot_of(target[0]))
    return scatter(acc)


def solution(mesh):
    return jax.shard_map(
        shards,
        mesh=mesh,
        in_specs=(
            P("grp", "blk", None, None, None),
            P("grp", "blk", None),
            P("grp", "blk", None, None, None),
            P("grp", "blk", None),
        ),
        out_specs=P("grp", "blk", None, None),
        check_vma=False,
    )
```

```python
import functools

import jax
import jax.numpy as jnp
from jax import lax
from jax.experimental import pallas as pl
from jax.experimental.pallas import tpu as pltpu
from jax.sharding import PartitionSpec as P

f32, bf16 = jnp.float32, jnp.bfloat16
MESH = pl.DeviceIdType.MESH

B = 96
LANES = 128
PACK = 72
KP = 2
KA = 27
FR = 24
MEMBERS = 8
GROUPS = 16
OWN = 4
SLOTS = 512
PARTS = 6
PIECE = OWN * PACK // PARTS
STEPS = 6

BITS = ("xg", "yg", "zg", "xh", "yh", "zh")


def bits_of(grp, blk):
    x, zl = blk % 4, blk // 4
    y, zh, core = grp // 4, (grp // 2) % 2, grp % 2
    xh, yh = x // 2, y // 2
    return {
        "xg": (xh + x % 2) % 2, "yg": (yh + y % 2) % 2, "zg": (zh + zl) % 2,
        "xh": xh, "yh": yh, "zh": zh, "core": core,
    }


def partner_of(grp, blk, bit):
    x, zl = blk % 4, blk // 4
    y, zh, core = grp // 4, (grp // 2) % 2, grp % 2
    if bit == "xg":
        x = x + 1 - 2 * (x % 2)
    elif bit == "xh":
        x = 3 - x
    elif bit == "yg":
        y = y + 1 - 2 * (y % 2)
    elif bit == "yh":
        y = 3 - y
    elif bit in ("zg", "zl"):
        zl = 1 - zl
    elif bit == "zh":
        zl, zh = 1 - zl, 1 - zh
    elif bit == "core":
        core = 1 - core
    return {"blk": zl * 4 + x, "grp": y * 4 + zh * 2 + core}


def order_of(part):
    return [BITS[(part + step) % STEPS] for step in range(STEPS)]


def slot_of(target):
    owner = target // OWN
    bits = bits_of(owner // MEMBERS, owner % MEMBERS)
    index = bits["core"]
    for bit in BITS:
        index = index * 2 + bits[bit]
    return index * OWN + target % OWN


def fold(main, tail):
    lane = lax.broadcasted_iota(jnp.int32, main.shape, 1)
    side = jnp.concatenate([pltpu.roll(tail, shift, 1) for shift in (96, 64, 32)], axis=0)
    return jnp.where(lane < B, main, side)


def unfold(packed):
    n = packed.shape[0] // 3
    lane = lax.broadcasted_iota(jnp.int32, (n, LANES), 1)
    first = pltpu.roll(packed[:n], 32, 1)
    second = pltpu.roll(packed[n:2 * n], 64, 1)
    third = pltpu.roll(packed[2 * n:], 96, 1)
    return jnp.where(lane < 32, first, jnp.where(lane < 64, second, third))


G_ORDERS = (("xg", "xh", "zl"), ("xh", "zl", "xg"), ("zl", "xg", "xh"))
G_PARTS = 3
G_ROWS = FR // G_PARTS
G_BATCH = 4


def member(part, blk, flip):
    x, zl = blk % 4, blk // 4
    xh = x // 2
    bits = {"xg": (xh + x % 2) % 2, "xh": xh, "zl": zl}
    index = 0
    for i, bit in enumerate(G_ORDERS[part]):
        if flip >> i & 1:
            bits[bit] = 1 - bits[bit]
        index = index + bits[bit] * (1 << i)
    return index, bits["zl"] * 4 + bits["xh"] * 2 + (bits["xh"] + bits["xg"]) % 2


def gather_kernel(p_hbm, out_ref, trans_ref, p_ref, landed, load_sem, send_sem, recv_sem):
    loads = []
    for part in range(G_PARTS):
        rows = pl.ds(part * G_ROWS, G_ROWS)
        load = pltpu.make_async_copy(p_hbm.at[rows], p_ref.at[rows], load_sem.at[part])
        load.start()
        loads.append(load)
    grp, blk = lax.axis_index("grp"), lax.axis_index("blk")
    partners = {bit: partner_of(grp, blk, bit) for bit in G_ORDERS[0]}
    barrier = pltpu.get_barrier_semaphore()
    for device in partners.values():
        pl.semaphore_signal(barrier, inc=1, device_id=device, device_id_type=MESH)
    where = [[member(part, blk, flip) for flip in range(MEMBERS)] for part in range(G_PARTS)]
    for part in range(G_PARTS):
        mine = where[part][0][0]
        loads[part].wait()

        for low in range(0, G_ROWS, G_BATCH):
            packed = []
            for r in range(low, low + G_BATCH):
                v = p_ref[part * G_ROWS + r].reshape(KP * B, B)
                v = jnp.pad(v, ((0, 0), (0, LANES - B)))
                packed.append(fold(v[:KP * PACK], v[KP * PACK:]))
            for r in range(G_BATCH):
                landed[part, mine, low + r] = packed[r]
    pl.semaphore_wait(barrier, len(partners))
    sends = []
    arrivals = {}

    def forward(part, flip, step):
        index = where[part][flip][0]
        copy = pltpu.make_async_remote_copy(
            src_ref=landed.at[part, index], dst_ref=landed.at[part, index],
            send_sem=send_sem.at[part, (1 << step) - 1 + flip], recv_sem=recv_sem.at[part, (1 << step) + flip],
            device_id=partners[G_ORDERS[part][step]], device_id_type=MESH)
        copy.start()
        sends.append(copy)
        arrivals[part, (1 << step) + flip] = copy

    def unpack(part, flip):
        index, source = where[part][flip]

        row = source * FR + part * G_ROWS
        for low in range(0, G_ROWS, G_BATCH):
            packed = [landed[part, index, low + r] for r in range(G_BATCH)]
            tails = [unfold(v) for v in packed]
            for r in range(G_BATCH):
                both = jnp.concatenate([packed[r], tails[r]], axis=0)
                for n in range(KP):
                    out_ref[row + low + r, :, n * LANES:(n + 1) * LANES] = both[n * B:(n + 1) * B]

    for step in range(3):
        for part in range(G_PARTS):
            forward(part, 0, step)
    for part in range(G_PARTS):
        unpack(part, 0)

    @pl.loop(0, FR)
    def _(r):
        for n in range(KP):
            trans_ref[r, n * B:(n + 1) * B, :] = p_ref[r, n].T
    for flip in range(1, MEMBERS):
        for part in range(G_PARTS):
            arrivals[part, flip].wait_recv()
            for step in range(flip.bit_length(), 3):
                forward(part, flip, step)
        for part in range(G_PARTS):
            unpack(part, flip)
    for copy in sends:
        copy.wait_send()


def gather(prolong):
    return pl.pallas_call(
        gather_kernel,
        out_shape=(
            jax.ShapeDtypeStruct((FR * MEMBERS, B, KP * LANES), bf16),
            jax.ShapeDtypeStruct((FR, KP * B, B), bf16)),
        in_specs=[pl.BlockSpec(memory_space=pl.ANY)],
        out_specs=(pl.BlockSpec(memory_space=pltpu.VMEM), pl.BlockSpec(memory_space=pltpu.VMEM)),
        scratch_shapes=[
            pltpu.VMEM((FR, KP, B, B), bf16),
            pltpu.VMEM((G_PARTS, MEMBERS, G_ROWS, KP * PACK, LANES), bf16),
            pltpu.SemaphoreType.DMA((G_PARTS,)),
            pltpu.SemaphoreType.DMA((G_PARTS, MEMBERS)), pltpu.SemaphoreType.DMA((G_PARTS, MEMBERS))],
        compiler_params=pltpu.CompilerParams(collective_id=0, has_side_effects=True, vmem_limit_bytes=20 << 20),
        name="gather_prolong",
    )(pltpu.with_memory_space_constraint(prolong, pltpu.HBM))


ROWS = 4
A_SLOTS = 8
AHEAD = 4


def product_kernel(col, tgt, a_ref, p_trans, chosen, acc, a_buf, a_sem):
    def fetch(i):
        slot = i % A_SLOTS
        return pltpu.make_async_copy(a_ref.at[i], a_buf.at[slot], a_sem.at[slot])

    for i in range(A_SLOTS - ROWS):
        fetch(i).start()

    @pl.loop(0, SLOTS // 8)
    def _(s):
        for j in range(8):
            acc[s * 8 + j] = jnp.zeros((B, LANES), f32)

    @pl.loop(0, FR // ROWS)
    def _(step):
        rows = [step * ROWS + r for r in range(ROWS)]
        for i in rows:
            fetch(i).wait()
        for i in rows:
            @pl.when(i + A_SLOTS - ROWS < FR)
            def _():
                fetch(i + A_SLOTS - ROWS).start()

        aps, values = {}, {}
        for u in range(ROWS * KA + 2 * AHEAD):
            if u < ROWS * KA:
                i, k = rows[u // KA], u % KA
                aps[u] = jnp.dot(a_buf[i % A_SLOTS, k], chosen[col[i, k]], preferred_element_type=f32).astype(bf16)
            v = u - AHEAD
            if 0 <= v < ROWS * KA:
                values[v] = jnp.dot(p_trans[rows[v // KA]], aps.pop(v), preferred_element_type=f32)
            w = v - AHEAD
            if w < 0:
                continue
            i, k = rows[w // KA], w % KA
            value = values.pop(w)
            for n in range(KP):
                for m in range(KP):
                    slot = tgt[i, n * (KA * KP) + k * KP + m]
                    acc[slot] += value[n * B:(n + 1) * B, m * LANES:(m + 1) * LANES]


def products(a_rows, columns, p_trans, chosen, slots):
    vmem = pl.BlockSpec(memory_space=pltpu.VMEM)
    smem = pl.BlockSpec(memory_space=pltpu.SMEM)
    return pl.pallas_call(
        product_kernel,
        out_shape=pltpu.VMEM((SLOTS, B, LANES), f32),
        in_specs=[smem, smem, pl.BlockSpec(memory_space=pl.ANY), vmem, vmem],
        out_specs=vmem,
        scratch_shapes=[
            pltpu.VMEM((A_SLOTS, KA, B, B), bf16),
            pltpu.SemaphoreType.DMA((A_SLOTS,))],
        compiler_params=pltpu.CompilerParams(vmem_limit_bytes=10 << 20),
        name="products",
    )(columns, slots, a_rows, p_trans, chosen)


BATCH = 16


def flipped(grp, blk, flips):
    place = {"grp": grp, "blk": blk}
    for bit in flips:
        place = partner_of(place["grp"], place["blk"], bit)
    return place


def direct(part, relative):
    return [bit for i, bit in enumerate(order_of(part)[3:]) if relative >> (2 - i) & 1]


def scatter_kernel(acc, out_ref, cross, other, keep0, give0, got0, keep1, give1, got1, keep2, give2, got2, last, arrived, total,
                   core_send, core_recv, send0, recv0, send1, recv1, send2, recv2, last_send, last_recv):
    grp, blk = lax.axis_index("grp"), lax.axis_index("blk")
    bits = bits_of(grp, blk)
    core = bits["core"]
    mine = [[bits[bit] for bit in order_of(part)] for part in range(PARTS)]
    lane = lax.broadcasted_iota(jnp.int32, (24, LANES), 1)
    flips = sorted({tuple(sorted(direct(part, r))) for part in range(PARTS) for r in range(1, 8)}) + [("core",)]
    partners = {f: flipped(grp, blk, f) for f in flips}

    def packed(part, side, entry):
        owner = side * 64 + entry % (1 << part) * (1 << (STEPS - part)) + entry // (1 << part)
        units = []
        for unit in (2 * (part % 3), 2 * (part % 3) + 1):
            j, u = part // 3 * 2 + unit // 3, unit % 3
            main = acc[owner * OWN + j, 24 * u:24 * u + 24]
            tail = acc[owner * OWN + j, PACK:]
            units.append(jnp.where(lane < B, main, pltpu.roll(tail, 96 - 32 * u, 1)))
        return jnp.concatenate(units, axis=0)

    def fill(target, n, value):
        def some(g, _):
            values = [value(g * batch + e).astype(target.dtype) for e in range(batch)]
            for e in range(batch):
                target[g * batch + e] = values[e]
            return 0
        batch = min(n, BATCH)
        lax.fori_loop(0, n // batch, some, 0)

    started = []

    def send(source, target, send_sem, recv_sem, device):
        copy = pltpu.make_async_remote_copy(
            src_ref=source, dst_ref=target, send_sem=send_sem, recv_sem=recv_sem,
            device_id=device, device_id_type=MESH)
        copy.start()
        started.append(copy)
        return copy

    barrier = pltpu.get_barrier_semaphore()
    for device in partners.values():
        pl.semaphore_signal(barrier, inc=1, device_id=device, device_id_type=MESH)

    crossed, first, second, third, final = {}, {}, {}, {}, {}
    def cross_over(part, chunk):
        offset = (1 - mine[part][0] if chunk == 0 else mine[part][0]) * 32
        fill(cross.at[part, chunk], 32, lambda e: packed(part, 1 - core, offset + e))
        if chunk == 0 and part == 0:
            pl.semaphore_wait(barrier, len(flips))
        crossed[part, chunk] = send(
            cross.at[part, chunk], other.at[part, chunk], core_send.at[part, chunk], core_recv.at[part, chunk],
            partners[("core",)])

    def give_away(part):
        crossed[part, 0].wait_recv()
        for chunk in range(2):
            offset = (1 - mine[part][1] if chunk == 0 else mine[part][1]) * 16
            away = (1 - mine[part][0]) * 32 + offset
            fill(give0.at[part, chunk], 16,
                 lambda e: packed(part, core, away + e) + other[part, 0, offset + e].astype(f32))
            first[part, chunk] = send(
                give0.at[part, chunk], got0.at[part, chunk], send0.at[part, chunk], recv0.at[part, chunk],
                partners[(order_of(part)[0],)])

    cross_over(0, 0)
    cross_over(1, 0)
    for part in range(PARTS):
        if part + 2 < PARTS:
            cross_over(part + 2, 0)
        give_away(part)
    for part in range(PARTS):
        cross_over(part, 1)
    for part in range(PARTS):
        crossed[part, 1].wait_recv()
        for chunk in range(2):
            offset = (1 - mine[part][1] if chunk == 0 else mine[part][1]) * 16
            here = mine[part][0] * 32 + offset
            fill(keep0.at[part, chunk], 16,
                 lambda e: packed(part, core, here + e) + other[part, 1, offset + e].astype(f32))

    for part in range(PARTS):
        first[part, 0].wait_recv()
        for chunk in range(2):
            offset = (1 - mine[part][2] if chunk == 0 else mine[part][2]) * 8
            fill(give1.at[part, chunk], 8,
                 lambda e: keep0[part, 0, offset + e] + got0[part, 0, offset + e].astype(f32))
            second[part, chunk] = send(
                give1.at[part, chunk], got1.at[part, chunk], send1.at[part, chunk], recv1.at[part, chunk],
                partners[(order_of(part)[1],)])
    for part in range(PARTS):
        first[part, 1].wait_recv()
        for chunk in range(2):
            offset = (1 - mine[part][2] if chunk == 0 else mine[part][2]) * 8
            fill(keep1.at[part, chunk], 8,
                 lambda e: keep0[part, 1, offset + e] + got0[part, 1, offset + e].astype(f32))

    for part in range(PARTS):
        second[part, 0].wait_recv()
        fill(give2.at[part], 8, lambda e: keep1[part, 0, e] + got1[part, 0, e].astype(f32))
        third[part] = send(
            give2.at[part], got2.at[part], send2.at[part], recv2.at[part], partners[(order_of(part)[2],)])
    for part in range(PARTS):
        second[part, 1].wait_recv()
        fill(keep2.at[part], 8, lambda e: keep1[part, 1, e] + got1[part, 1, e].astype(f32))

    for part in range(PARTS):
        third[part].wait_recv()
        for r in range(8):
            entry = 0
            for i in range(3):
                bit = mine[part][3 + i]
                entry = entry * 2 + (1 - bit if r >> (2 - i) & 1 else bit)
            value = keep2[part, entry] + got2[part, entry].astype(f32)
            if r == 0:
                total[part] = value
                continue
            last[part, r - 1] = value.astype(bf16)
            final[part, r] = send(
                last.at[part, r - 1], arrived.at[part, r - 1], last_send.at[part, r - 1], last_recv.at[part, r - 1],
                partners[tuple(sorted(direct(part, r)))])
    pieces = []
    for part in range(PARTS):
        value = total[part]
        for r in range(1, 8):
            final[part, r].wait_recv()
            value = value + arrived[part, r - 1].astype(f32)
        pieces.append(value)
    for pair in range(2):
        both = jnp.concatenate(pieces[pair * 3:pair * 3 + 3], axis=0)
        for j in range(2):
            block = both[j * PACK:(j + 1) * PACK]
            out_ref[0, pair * 2 + j, :PACK] = block[:, :B]
            out_ref[0, pair * 2 + j, PACK:] = unfold(block)[:, :B]
    for copy in started:
        copy.wait_send()


def scatter(acc):
    def piece(dtype, *lead):
        return pltpu.VMEM((PARTS,) + lead + (PIECE, LANES), dtype)
    dma = pltpu.SemaphoreType.DMA
    return pl.pallas_call(
        scatter_kernel,
        out_shape=pltpu.VMEM((1, OWN, B, B), f32),
        in_specs=[pl.BlockSpec(memory_space=pltpu.VMEM)],
        out_specs=pl.BlockSpec(memory_space=pltpu.VMEM),
        scratch_shapes=[
            piece(bf16, 2, 32), piece(bf16, 2, 32),
            piece(f32, 2, 16), piece(bf16, 2, 16), piece(bf16, 2, 16),
            piece(f32, 2, 8), piece(bf16, 2, 8), piece(bf16, 2, 8),
            piece(f32, 8), piece(bf16, 8), piece(bf16, 8),
            piece(bf16, 7), piece(bf16, 7), piece(f32)]
            + [dma((PARTS, 2))] * 6 + [dma((PARTS,))] * 2 + [dma((PARTS, 7))] * 2,
        compiler_params=pltpu.CompilerParams(collective_id=1, has_side_effects=True, vmem_limit_bytes=30 << 20),
        name="sum_at_owners",
    )(pltpu.with_memory_space_constraint(acc, pltpu.VMEM))


def shards(a_blocks, col_index, prolong, target):
    chosen, p_trans = gather(prolong[0])
    acc = products(a_blocks[0], col_index[0], p_trans, chosen, slot_of(target[0]))
    return scatter(acc)


def solution(mesh):
    return jax.shard_map(
        shards,
        mesh=mesh,
        in_specs=(
            P("grp", "blk", None, None, None),
            P("grp", "blk", None),
            P("grp", "blk", None, None, None),
            P("grp", "blk", None),
        ),
        out_specs=P("grp", "blk", None, None),
        check_vma=False,
    )
```

```python
import functools

import jax
import jax.numpy as jnp
from jax import lax
from jax.experimental import pallas as pl
from jax.experimental.pallas import tpu as pltpu
from jax.sharding import PartitionSpec as P

f32, bf16 = jnp.float32, jnp.bfloat16
MESH = pl.DeviceIdType.MESH

B = 96
LANES = 128
PACK = 72
KP = 2
KA = 27
FR = 24
MEMBERS = 8
GROUPS = 16
OWN = 4
SLOTS = 512
PARTS = 6
PIECE = OWN * PACK // PARTS
STEPS = 6

BITS = ("xg", "yg", "zg", "xh", "yh", "zh")


def bits_of(grp, blk):
    x, zl = blk % 4, blk // 4
    y, zh, core = grp // 4, (grp // 2) % 2, grp % 2
    xh, yh = x // 2, y // 2
    return {
        "xg": (xh + x % 2) % 2, "yg": (yh + y % 2) % 2, "zg": (zh + zl) % 2,
        "xh": xh, "yh": yh, "zh": zh, "core": core,
    }


def partner_of(grp, blk, bit):
    x, zl = blk % 4, blk // 4
    y, zh, core = grp // 4, (grp // 2) % 2, grp % 2
    if bit == "xg":
        x = x + 1 - 2 * (x % 2)
    elif bit == "xh":
        x = 3 - x
    elif bit == "yg":
        y = y + 1 - 2 * (y % 2)
    elif bit == "yh":
        y = 3 - y
    elif bit in ("zg", "zl"):
        zl = 1 - zl
    elif bit == "zh":
        zl, zh = 1 - zl, 1 - zh
    elif bit == "core":
        core = 1 - core
    return {"blk": zl * 4 + x, "grp": y * 4 + zh * 2 + core}


def order_of(part):
    return [BITS[(part + step) % STEPS] for step in range(STEPS)]


def slot_of(target):
    blk, grp = target >> 2 & 7, target >> 5
    zl, zh, xh, yh = blk >> 2, grp >> 1 & 1, blk >> 1 & 1, grp >> 3
    bits = (grp & 1, xh ^ (blk & 1), yh ^ (grp >> 2 & 1), zh ^ zl, xh, yh, zh)
    index = bits[0]
    for bit in bits[1:]:
        index = index << 1 | bit
    return index << 2 | target & 3


def fold(main, tail):
    lane = lax.broadcasted_iota(jnp.int32, main.shape, 1)
    side = jnp.concatenate([pltpu.roll(tail, shift, 1) for shift in (96, 64, 32)], axis=0)
    return jnp.where(lane < B, main, side)


def unfold(packed):
    n = packed.shape[0] // 3
    lane = lax.broadcasted_iota(jnp.int32, (n, LANES), 1)
    first = pltpu.roll(packed[:n], 32, 1)
    second = pltpu.roll(packed[n:2 * n], 64, 1)
    third = pltpu.roll(packed[2 * n:], 96, 1)
    return jnp.where(lane < 32, first, jnp.where(lane < 64, second, third))


G_ORDERS = (("xg", "xh", "zl"), ("xh", "zl", "xg"), ("zl", "xg", "xh"))
G_PARTS = 3
G_ROWS = FR // G_PARTS
G_BATCH = 4


def member(part, blk, flip):
    x, zl = blk % 4, blk // 4
    xh = x // 2
    bits = {"xg": (xh + x % 2) % 2, "xh": xh, "zl": zl}
    index = 0
    for i, bit in enumerate(G_ORDERS[part]):
        if flip >> i & 1:
            bits[bit] = 1 - bits[bit]
        index = index + bits[bit] * (1 << i)
    return index, bits["zl"] * 4 + bits["xh"] * 2 + (bits["xh"] + bits["xg"]) % 2


def gather_kernel(p_hbm, c_hbm, t_hbm, out_ref, trans_ref, c_ref, s_ref, p_ref, landed, t_ref, table_sem, load_sem, send_sem, recv_sem):
    tables = [pltpu.make_async_copy(c_hbm, c_ref, table_sem.at[0]), pltpu.make_async_copy(t_hbm, t_ref, table_sem.at[1])]
    loads = []
    for part in range(G_PARTS):
        rows = pl.ds(part * G_ROWS, G_ROWS)
        load = pltpu.make_async_copy(p_hbm.at[rows], p_ref.at[rows], load_sem.at[part])
        load.start()
        loads.append(load)
    for table in tables:
        table.start()
    grp, blk = lax.axis_index("grp"), lax.axis_index("blk")
    partners = {bit: partner_of(grp, blk, bit) for bit in G_ORDERS[0]}
    barrier = pltpu.get_barrier_semaphore()
    for device in partners.values():
        pl.semaphore_signal(barrier, inc=1, device_id=device, device_id_type=MESH)
    where = [[member(part, blk, flip) for flip in range(MEMBERS)] for part in range(G_PARTS)]
    for part in range(G_PARTS):
        mine = where[part][0][0]
        loads[part].wait()

        for low in range(0, G_ROWS, G_BATCH):
            packed = []
            for r in range(low, low + G_BATCH):
                v = p_ref[part * G_ROWS + r].reshape(KP * B, B)
                v = jnp.pad(v, ((0, 0), (0, LANES - B)))
                packed.append(fold(v[:KP * PACK], v[KP * PACK:]))
            for r in range(G_BATCH):
                landed[part, mine, low + r] = packed[r]
    pl.semaphore_wait(barrier, len(partners))
    sends = []
    arrivals = {}

    def forward(part, flip, step):
        index = where[part][flip][0]
        copy = pltpu.make_async_remote_copy(
            src_ref=landed.at[part, index], dst_ref=landed.at[part, index],
            send_sem=send_sem.at[part, (1 << step) - 1 + flip], recv_sem=recv_sem.at[part, (1 << step) + flip],
            device_id=partners[G_ORDERS[part][step]], device_id_type=MESH)
        copy.start()
        sends.append(copy)
        arrivals[part, (1 << step) + flip] = copy

    def unpack(part, flip):
        index, source = where[part][flip]

        row = source * FR + part * G_ROWS
        for low in range(0, G_ROWS, G_BATCH):
            packed = [landed[part, index, low + r] for r in range(G_BATCH)]
            tails = [unfold(v) for v in packed]
            for r in range(G_BATCH):
                both = jnp.concatenate([packed[r], tails[r]], axis=0)
                for n in range(KP):
                    out_ref[row + low + r, :, n * LANES:(n + 1) * LANES] = both[n * B:(n + 1) * B]

    for step in range(3):
        for part in range(G_PARTS):
            forward(part, 0, step)
    for part in range(G_PARTS):
        unpack(part, 0)

    @pl.loop(0, FR)
    def _(r):
        for n in range(KP):
            trans_ref[r, n * B:(n + 1) * B, :] = p_ref[r, n].T

    for table in tables:
        table.wait()
    s_ref[...] = slot_of(t_ref[...])
    for flip in range(1, MEMBERS):
        for part in range(G_PARTS):
            arrivals[part, flip].wait_recv()
            for step in range(flip.bit_length(), 3):
                forward(part, flip, step)
        for part in range(G_PARTS):
            unpack(part, flip)
    for copy in sends:
        copy.wait_send()


def gather(prolong, columns, targets):
    return pl.pallas_call(
        gather_kernel,
        out_shape=(
            jax.ShapeDtypeStruct((FR * MEMBERS, B, KP * LANES), bf16),
            jax.ShapeDtypeStruct((FR, KP * B, B), bf16),
            jax.ShapeDtypeStruct(columns.shape, jnp.int32),
            jax.ShapeDtypeStruct(targets.shape, jnp.int32)),
        in_specs=[pl.BlockSpec(memory_space=pl.ANY)] * 3,
        out_specs=(pl.BlockSpec(memory_space=pltpu.VMEM),) * 4,
        scratch_shapes=[
            pltpu.VMEM((FR, KP, B, B), bf16),
            pltpu.VMEM((G_PARTS, MEMBERS, G_ROWS, KP * PACK, LANES), bf16),
            pltpu.VMEM(targets.shape, jnp.int32),
            pltpu.SemaphoreType.DMA((2,)), pltpu.SemaphoreType.DMA((G_PARTS,)),
            pltpu.SemaphoreType.DMA((G_PARTS, MEMBERS)), pltpu.SemaphoreType.DMA((G_PARTS, MEMBERS))],
        compiler_params=pltpu.CompilerParams(collective_id=0, has_side_effects=True, vmem_limit_bytes=20 << 20),
        name="gather_prolong",
    )(*(pltpu.with_memory_space_constraint(v, pltpu.HBM) for v in (prolong, columns, targets)))


ROWS = 4
A_SLOTS = 8
AHEAD = 4


def product_kernel(col, tgt, a_ref, p_trans, chosen, acc, a_buf, a_sem):
    def fetch(i):
        slot = i % A_SLOTS
        return pltpu.make_async_copy(a_ref.at[i], a_buf.at[slot], a_sem.at[slot])

    for i in range(A_SLOTS - ROWS):
        fetch(i).start()

    @pl.loop(0, SLOTS // 8)
    def _(s):
        for j in range(8):
            acc[s * 8 + j] = jnp.zeros((B, LANES), f32)

    @pl.loop(0, FR // ROWS)
    def _(step):
        rows = [step * ROWS + r for r in range(ROWS)]
        for i in rows:
            fetch(i).wait()
        for i in rows:
            @pl.when(i + A_SLOTS - ROWS < FR)
            def _():
                fetch(i + A_SLOTS - ROWS).start()

        aps, values = {}, {}
        for u in range(ROWS * KA + 2 * AHEAD):
            if u < ROWS * KA:
                i, k = rows[u // KA], u % KA
                aps[u] = jnp.dot(a_buf[i % A_SLOTS, k], chosen[col[i, k]], preferred_element_type=f32).astype(bf16)
            v = u - AHEAD
            if 0 <= v < ROWS * KA:
                values[v] = jnp.dot(p_trans[rows[v // KA]], aps.pop(v), preferred_element_type=f32)
            w = v - AHEAD
            if w < 0:
                continue
            i, k = rows[w // KA], w % KA
            value = values.pop(w)
            for n in range(KP):
                for m in range(KP):
                    slot = tgt[i, n * (KA * KP) + k * KP + m]
                    acc[slot] += value[n * B:(n + 1) * B, m * LANES:(m + 1) * LANES]


def products(a_rows, columns, p_trans, chosen, slots):
    vmem = pl.BlockSpec(memory_space=pltpu.VMEM)
    smem = pl.BlockSpec(memory_space=pltpu.SMEM)
    return pl.pallas_call(
        product_kernel,
        out_shape=pltpu.VMEM((SLOTS, B, LANES), f32),
        in_specs=[smem, smem, pl.BlockSpec(memory_space=pl.ANY), vmem, vmem],
        out_specs=vmem,
        scratch_shapes=[
            pltpu.VMEM((A_SLOTS, KA, B, B), bf16),
            pltpu.SemaphoreType.DMA((A_SLOTS,))],
        compiler_params=pltpu.CompilerParams(vmem_limit_bytes=10 << 20),
        name="products",
    )(columns, slots, a_rows, p_trans, chosen)


BATCH = 16


def flipped(grp, blk, flips):
    place = {"grp": grp, "blk": blk}
    for bit in flips:
        place = partner_of(place["grp"], place["blk"], bit)
    return place


def direct(part, relative):
    return [bit for i, bit in enumerate(order_of(part)[3:]) if relative >> (2 - i) & 1]


def scatter_kernel(acc, out_ref, cross, other, keep0, give0, got0, keep1, give1, got1, keep2, give2, got2, last, arrived, total,
                   core_send, core_recv, send0, recv0, send1, recv1, send2, recv2, last_send, last_recv):
    grp, blk = lax.axis_index("grp"), lax.axis_index("blk")
    bits = bits_of(grp, blk)
    core = bits["core"]
    mine = [[bits[bit] for bit in order_of(part)] for part in range(PARTS)]
    lane = lax.broadcasted_iota(jnp.int32, (24, LANES), 1)
    flips = sorted({tuple(sorted(direct(part, r))) for part in range(PARTS) for r in range(1, 8)}) + [("core",)]
    partners = {f: flipped(grp, blk, f) for f in flips}

    def packed(part, side, entry):
        owner = side * 64 + entry % (1 << part) * (1 << (STEPS - part)) + entry // (1 << part)
        units = []
        for unit in (2 * (part % 3), 2 * (part % 3) + 1):
            j, u = part // 3 * 2 + unit // 3, unit % 3
            main = acc[owner * OWN + j, 24 * u:24 * u + 24]
            tail = acc[owner * OWN + j, PACK:]
            units.append(jnp.where(lane < B, main, pltpu.roll(tail, 96 - 32 * u, 1)))
        return jnp.concatenate(units, axis=0)

    def fill(target, n, value):
        def some(g, _):
            values = [value(g * batch + e).astype(target.dtype) for e in range(batch)]
            for e in range(batch):
                target[g * batch + e] = values[e]
            return 0
        batch = min(n, BATCH)
        lax.fori_loop(0, n // batch, some, 0)

    started = []

    def send(source, target, send_sem, recv_sem, device):
        copy = pltpu.make_async_remote_copy(
            src_ref=source, dst_ref=target, send_sem=send_sem, recv_sem=recv_sem,
            device_id=device, device_id_type=MESH)
        copy.start()
        started.append(copy)
        return copy

    barrier = pltpu.get_barrier_semaphore()
    for device in partners.values():
        pl.semaphore_signal(barrier, inc=1, device_id=device, device_id_type=MESH)

    crossed, first, second, third, final = {}, {}, {}, {}, {}
    def pack(part, chunk):
        offset = (1 - mine[part][0] if chunk == 0 else mine[part][0]) * 32
        fill(cross.at[part, chunk], 32, lambda e: packed(part, 1 - core, offset + e))

    def cross_over(part, chunk):
        crossed[part, chunk] = send(
            cross.at[part, chunk], other.at[part, chunk], core_send.at[part, chunk], core_recv.at[part, chunk],
            partners[("core",)])

    def give_away(part, chunk):
        offset = (1 - mine[part][1] if chunk == 0 else mine[part][1]) * 16
        away = (1 - mine[part][0]) * 32 + offset
        fill(give0.at[part, chunk], 16,
             lambda e: packed(part, core, away + e) + other[part, 0, offset + e].astype(f32))
        first[part, chunk] = send(
            give0.at[part, chunk], got0.at[part, chunk], send0.at[part, chunk], recv0.at[part, chunk],
            partners[(order_of(part)[0],)])

    for part in range(PARTS):
        pack(part, 0)
    pl.semaphore_wait(barrier, len(flips))
    for part in range(PARTS):
        cross_over(part, 0)
    for part in range(PARTS):
        crossed[part, 0].wait_recv()
        give_away(part, 0)
    for part in range(PARTS):
        give_away(part, 1)
    for part in range(PARTS):
        pack(part, 1)
        cross_over(part, 1)
    for part in range(PARTS):
        crossed[part, 1].wait_recv()
        for chunk in range(2):
            offset = (1 - mine[part][1] if chunk == 0 else mine[part][1]) * 16
            here = mine[part][0] * 32 + offset
            fill(keep0.at[part, chunk], 16,
                 lambda e: packed(part, core, here + e) + other[part, 1, offset + e].astype(f32))

    for part in range(PARTS):
        first[part, 0].wait_recv()
        for chunk in range(2):
            offset = (1 - mine[part][2] if chunk == 0 else mine[part][2]) * 8
            fill(give1.at[part, chunk], 8,
                 lambda e: keep0[part, 0, offset + e] + got0[part, 0, offset + e].astype(f32))
            second[part, chunk] = send(
                give1.at[part, chunk], got1.at[part, chunk], send1.at[part, chunk], recv1.at[part, chunk],
                partners[(order_of(part)[1],)])
    for part in range(PARTS):
        first[part, 1].wait_recv()
        for chunk in range(2):
            offset = (1 - mine[part][2] if chunk == 0 else mine[part][2]) * 8
            fill(keep1.at[part, chunk], 8,
                 lambda e: keep0[part, 1, offset + e] + got0[part, 1, offset + e].astype(f32))

    for part in range(PARTS):
        second[part, 0].wait_recv()
        fill(give2.at[part], 8, lambda e: keep1[part, 0, e] + got1[part, 0, e].astype(f32))
        third[part] = send(
            give2.at[part], got2.at[part], send2.at[part], recv2.at[part], partners[(order_of(part)[2],)])
    for part in range(PARTS):
        second[part, 1].wait_recv()
        fill(keep2.at[part], 8, lambda e: keep1[part, 1, e] + got1[part, 1, e].astype(f32))

    for part in range(PARTS):
        third[part].wait_recv()
        values = []
        for r in range(8):
            entry = 0
            for i in range(3):
                bit = mine[part][3 + i]
                entry = entry * 2 + (1 - bit if r >> (2 - i) & 1 else bit)
            values.append(keep2[part, entry] + got2[part, entry].astype(f32))
        total[part] = values[0]
        for r in range(1, 8):
            last[part, r - 1] = values[r].astype(bf16)
        for r in range(1, 8):
            final[part, r] = send(
                last.at[part, r - 1], arrived.at[part, r - 1], last_send.at[part, r - 1], last_recv.at[part, r - 1],
                partners[tuple(sorted(direct(part, r)))])
    pieces = []
    for part in range(PARTS):
        value = total[part]
        for r in range(1, 8):
            final[part, r].wait_recv()
            value = value + arrived[part, r - 1].astype(f32)
        pieces.append(value)
    for pair in range(2):
        both = jnp.concatenate(pieces[pair * 3:pair * 3 + 3], axis=0)
        for j in range(2):
            block = both[j * PACK:(j + 1) * PACK]
            out_ref[0, pair * 2 + j, :PACK] = block[:, :B]
            out_ref[0, pair * 2 + j, PACK:] = unfold(block)[:, :B]
    for copy in started:
        copy.wait_send()


def scatter(acc):
    def piece(dtype, *lead):
        return pltpu.VMEM((PARTS,) + lead + (PIECE, LANES), dtype)
    dma = pltpu.SemaphoreType.DMA
    return pl.pallas_call(
        scatter_kernel,
        out_shape=pltpu.VMEM((1, OWN, B, B), f32),
        in_specs=[pl.BlockSpec(memory_space=pltpu.VMEM)],
        out_specs=pl.BlockSpec(memory_space=pltpu.VMEM),
        scratch_shapes=[
            piece(bf16, 2, 32), piece(bf16, 2, 32),
            piece(f32, 2, 16), piece(bf16, 2, 16), piece(bf16, 2, 16),
            piece(f32, 2, 8), piece(bf16, 2, 8), piece(bf16, 2, 8),
            piece(f32, 8), piece(bf16, 8), piece(bf16, 8),
            piece(bf16, 7), piece(bf16, 7), piece(f32)]
            + [dma((PARTS, 2))] * 6 + [dma((PARTS,))] * 2 + [dma((PARTS, 7))] * 2,
        compiler_params=pltpu.CompilerParams(collective_id=1, has_side_effects=True, vmem_limit_bytes=30 << 20),
        name="sum_at_owners",
    )(pltpu.with_memory_space_constraint(acc, pltpu.VMEM))


def shards(a_blocks, col_index, prolong, target):
    chosen, p_trans, columns, slots = gather(prolong[0], col_index[0], target[0])
    acc = products(a_blocks[0], columns, p_trans, chosen, slots)
    return scatter(acc)


def solution(mesh):
    return jax.shard_map(
        shards,
        mesh=mesh,
        in_specs=(
            P("grp", "blk", None, None, None),
            P("grp", "blk", None),
            P("grp", "blk", None, None, None),
            P("grp", "blk", None),
        ),
        out_specs=P("grp", "blk", None, None),
        check_vma=False,
    )
```
